32 devices in a mesh: fsdp: 8 (over y, x, core), shard: 4 (over z).
Axes of the slice: x: 2, y: 2, z: 4, core: 2. Of those that a mesh axis runs over, the one named last changes fastest.
Arguments:
- tokens: bfloat16 [4096, 1024], P(('fsdp', 'shard')), may hold values from -6 to 6
- cotangent: bfloat16 [4096, 1024], P(('fsdp', 'shard')), may hold values from -6 to 6
- starts: int32 [4096], P(('fsdp', 'shard')), may hold values from 0 to 127, as said below
- counts: int32 [32], P(('fsdp', 'shard')), may hold values from 64 to 128, as said below
- attn_gain: bfloat16 [4, 256], P('shard', 'fsdp'), may hold values from 0.5 to 1.5
- attn_shift: bfloat16 [4, 256], P('shard', 'fsdp'), may hold values from -1.75 to 1.75
- w_qkv: bfloat16 [1024, 3, 1024], P('fsdp', None, 'shard'), may hold values from -0.1875 to 0.1875
- query_bias: bfloat16 [4, 256], P('shard', 'fsdp'), may hold values from -1.75 to 1.75
- value_bias: bfloat16 [4, 256], P('shard', 'fsdp'), may hold values from -1.75 to 1.75
- w_proj: bfloat16 [1024, 1024], P('shard', 'fsdp'), may hold values from -0.75 to 0.75
- proj_bias: bfloat16 [4, 256], P('shard', 'fsdp'), may hold values from -1.75 to 1.75
- mlp_gain: bfloat16 [4, 256], P('shard', 'fsdp'), may hold values from 0.5 to 1.5
- mlp_shift: bfloat16 [4, 256], P('shard', 'fsdp'), may hold values from -1.75 to 1.75
- w_up: bfloat16 [1024, 4096], P('fsdp', 'shard'), may hold values from -0.1875 to 0.1875
- up_bias: bfloat16 [4, 1024], P('shard', 'fsdp'), may hold values from -1.75 to 1.75
- w_down: bfloat16 [4096, 1024], P('shard', 'fsdp'), may hold values from -0.375 to 0.375
- down_bias: bfloat16 [4, 256], P('shard', 'fsdp'), may hold values from -1.75 to 1.75
Outputs:
- block_out: bfloat16 [4096, 1024], P(('fsdp', 'shard'))
- grad_tokens: float32 [4096, 1024], P(('fsdp', 'shard'))
- grad_attn_gain: float32 [4, 256], P('shard', 'fsdp')
- grad_attn_shift: float32 [4, 256], P('shard', 'fsdp')
- grad_w_qkv: float32 [1024, 3, 1024], P('fsdp', None, 'shard')
- grad_query_bias: float32 [4, 256], P('shard', 'fsdp')
- grad_value_bias: float32 [4, 256], P('shard', 'fsdp')
- grad_w_proj: float32 [1024, 1024], P('shard', 'fsdp')
- grad_proj_bias: float32 [4, 256], P('shard', 'fsdp')
- grad_mlp_gain: float32 [4, 256], P('shard', 'fsdp')
- grad_mlp_shift: float32 [4, 256], P('shard', 'fsdp')
- grad_w_up: float32 [1024, 4096], P('fsdp', 'shard')
- grad_up_bias: float32 [4, 1024], P('shard', 'fsdp')
- grad_w_down: float32 [4096, 1024], P('shard', 'fsdp')
- grad_down_bias: float32 [4, 256], P('shard', 'fsdp')
The draws below stay inside these ranges and needn't reach their ends.
Inputs may be any that keep to these rules, and one draw needn't show every extreme that they name: starts[s] is the index, inside the block of 128 slots that holds slot s, of the first slot of s's sequence; a sequence's slots are consecutive in one block and never cross blocks; slots at or past the block's live count start themselves; in every draw some block holds one sequence over all 128 slots. The live slots are the first counts[b] of block b; some block is full in every draw.
All inputs are finite; a program needn't handle non-finite values.
Results may differ from the reference program's by a relative error of at most 0.012.
Values may be sent and summed in bfloat16 or wider, within the bound.
No kernel may reach another device: no remote copies, remote signals or barrier semaphores. Data moves between devices by JAX's collectives and lax.ppermute only.
A program may use at most 128 MiB of HBM per device.

```python
import jax
import jax.numpy as jnp
from jax import lax

D = 1024
FF = 4096
HEAD_DIM = 64
CAP = 128
SLOTS = 4096
N_FSDP = 8
N_SHARD = 4


def layout_ints(key):
    block_count = SLOTS // CAP
    live_counts = jax.random.randint(jax.random.fold_in(key, 11), (block_count,), CAP // 2, CAP + 1, dtype=jnp.int32)
    full_block = jax.random.randint(jax.random.fold_in(key, 12), (), 0, block_count, dtype=jnp.int32)
    block_ids = jnp.arange(block_count, dtype=jnp.int32)
    live_counts = jnp.where(block_ids == full_block, CAP, live_counts)
    positions = jnp.arange(CAP, dtype=jnp.int32)
    cut_marks = jax.random.randint(jax.random.fold_in(key, 13), (block_count, CAP), 0, 24, dtype=jnp.int32) == 0
    boundary = cut_marks | (positions[None, :] == 0) | (positions[None, :] >= live_counts[:, None])
    boundary = jnp.where((block_ids == full_block)[:, None], positions[None, :] == 0, boundary)
    first_slots = lax.cummax(jnp.where(boundary, positions[None, :], 0), axis=1)
    return (first_slots.reshape(block_count * CAP), live_counts)


def draw_starts(key, part):
    return layout_ints(key)[0]


def draw_counts(key, part):
    return layout_ints(key)[1]


def with_spikes(drawn, own_key, source, target, blocks, factor):
    owner, partner = [(jnp.arange(drawn.shape[dim]) // (drawn.shape[dim] // blocks)).reshape([-1 if axis == dim else 1 for axis in range(drawn.ndim)]) for dim in (source, target)]
    chosen = jax.random.permutation(own_key, blocks)[partner]
    strong = (owner == chosen) | (owner == (partner + blocks // 2) % blocks)
    return jnp.where(strong, factor * drawn, drawn)


def level_of(stream_key, shape, shards, low, high):
    gain, own = 1.0, jax.random.fold_in(stream_key, 6)
    for dim, parts in shards:
        draws = jnp.exp(jax.random.uniform(jax.random.fold_in(own, dim), (parts,), jnp.float32, low / len(shards), high / len(shards)))
        gain = gain * jnp.repeat(draws, shape[dim] // parts).reshape([-1 if axis == dim else 1 for axis in range(len(shape))])
    return gain


def scatter_about(key, extent, scale, most, cuts=(), kind=jnp.bfloat16):
    array = scale * jax.random.normal(key, extent, jnp.float32)
    if cuts:
        array = array * level_of(key, extent, cuts, -0.22, 0.18)
    return jnp.clip(array, -most, most).astype(kind)


def bell_draw_with(rng, extent, spread, reach, cuts, heavy, kind=jnp.bfloat16):
    array = spread * jax.random.normal(rng, extent, jnp.float32)
    if cuts:
        array = array * level_of(rng, extent, cuts, -0.22, 0.18)
    return jnp.clip(with_spikes(array, jax.random.fold_in(rng, 3), *heavy), -reach, reach).astype(kind)


def setup_inputs(seed: int = 0) -> dict:
    splits = jax.random.split(jax.random.key(seed), 18)
    tokens = bell_draw_with(splits[0], (SLOTS, D), 1.0, 6.0, ((0, 32),), (0, 1, 32, 2.75))
    cotangent = bell_draw_with(splits[1], (SLOTS, D), 1.0, 6.0, ((0, 32),), (0, 1, 32, 2.75))
    starts = draw_starts(jax.random.fold_in(splits[17], 71), 0)
    counts = draw_counts(jax.random.fold_in(splits[17], 71), 0)
    attn_gain = jnp.clip(1.0 + 0.1 * jax.random.normal(splits[4], (N_SHARD, D // N_SHARD), jnp.float32), 0.5, 1.5).astype(jnp.bfloat16)
    attn_shift = scatter_about(splits[5], (N_SHARD, D // N_SHARD), 0.3, 1.75, ((0, 4), (1, 8)))
    w_qkv = scatter_about(splits[6], (D, 3, D), D ** -0.5, 0.1875, ((0, 8), (2, 4)))
    query_bias = scatter_about(splits[7], (N_SHARD, D // N_SHARD), 0.3, 1.75, ((0, 4), (1, 8)))
    value_bias = scatter_about(splits[8], (N_SHARD, D // N_SHARD), 0.3, 1.75, ((0, 4), (1, 8)))
    w_proj = scatter_about(splits[9], (D, D), (D // 16) ** -0.5, 0.75, ((0, 4), (1, 8)))
    proj_bias = scatter_about(splits[10], (N_SHARD, D // N_SHARD), 0.3, 1.75, ((0, 4), (1, 8)))
    mlp_gain = jnp.clip(1.0 + 0.1 * jax.random.normal(splits[11], (N_SHARD, D // N_SHARD), jnp.float32), 0.5, 1.5).astype(jnp.bfloat16)
    mlp_shift = scatter_about(splits[12], (N_SHARD, D // N_SHARD), 0.3, 1.75, ((0, 4), (1, 8)))
    w_up = scatter_about(splits[13], (D, FF), D ** -0.5, 0.1875, ((0, 8), (1, 4)))
    up_bias = scatter_about(splits[14], (N_SHARD, FF // N_SHARD), 0.3, 1.75, ((0, 4), (1, 8)))
    w_down = scatter_about(splits[15], (FF, D), (FF // 16) ** -0.5, 0.375, ((0, 4), (1, 8)))
    down_bias = scatter_about(splits[16], (N_SHARD, D // N_SHARD), 0.3, 1.75, ((0, 4), (1, 8)))
    return dict(tokens=tokens, cotangent=cotangent, starts=starts, counts=counts, attn_gain=attn_gain, attn_shift=attn_shift, w_qkv=w_qkv, query_bias=query_bias, value_bias=value_bias, w_proj=w_proj, proj_bias=proj_bias, mlp_gain=mlp_gain, mlp_shift=mlp_shift, w_up=w_up, up_bias=up_bias, w_down=w_down, down_bias=down_bias)


NORM_EPS = 1e-05
NEG_FILL = -1e+30

def layer_norm(inputs, norm_gain, norm_shift):
    center = inputs - lax.optimization_barrier(jnp.mean(inputs, axis=-1, keepdims=True))
    variance = lax.optimization_barrier(jnp.mean(center * center, axis=-1, keepdims=True))
    return center * lax.rsqrt(variance + NORM_EPS) * norm_gain + norm_shift

def gelu_tanh(values):
    return jax.nn.gelu(values, approximate=True)

def split_heads(qkv_full, width):
    slot_count = qkv_full.shape[0]
    head_count = width // HEAD_DIM
    query_part = qkv_full[:, :width].reshape(slot_count, head_count, HEAD_DIM)
    key_part = qkv_full[:, width:2 * width].reshape(slot_count, head_count, HEAD_DIM)
    value_part = qkv_full[:, 2 * width:].reshape(slot_count, head_count, HEAD_DIM)
    return (query_part, key_part, value_part)

def score_block(query_part, key_part, starts_blk):
    scores = jnp.einsum('qhd,khd->hqk', query_part.astype(jnp.float32), key_part.astype(jnp.float32))
    scores = scores * HEAD_DIM ** (-0.5)
    positions = jnp.arange(scores.shape[1], dtype=jnp.int32)
    visible = (positions[None, :] >= starts_blk[:, None]) & (positions[None, :] <= positions[:, None])
    return jnp.where(visible[None], scores, NEG_FILL)

def forward_pass(full, tokens_blk, starts_blk, live):
    attn_gain, attn_shift, w_qkv, query_bias, value_bias, w_proj, proj_bias, mlp_gain, mlp_shift, w_up, up_bias, w_down, down_bias = full
    slot_count = tokens_blk.shape[0]
    width = tokens_blk.shape[1]
    tokens_wide = tokens_blk.astype(jnp.float32)
    normed_attn = layer_norm(tokens_wide, attn_gain.astype(jnp.float32), attn_shift.astype(jnp.float32))
    act_attn = normed_attn.astype(jnp.bfloat16)
    qkv_bias = jnp.concatenate([query_bias, jnp.zeros_like(query_bias), value_bias]).astype(jnp.float32)
    qkv_full = (jnp.dot(act_attn, w_qkv, preferred_element_type=jnp.float32) + qkv_bias).astype(jnp.bfloat16)
    query_part, key_part, value_part = split_heads(qkv_full, width)
    scores = score_block(query_part, key_part, starts_blk)
    row_max = lax.optimization_barrier(jnp.max(scores, axis=-1, keepdims=True))
    log_total = row_max + jnp.log(lax.optimization_barrier(jnp.sum(jnp.exp(scores - row_max), axis=-1, keepdims=True)))
    probs_low = jnp.exp(scores - log_total).astype(jnp.bfloat16)
    mixed = jnp.einsum('hqk,khd->qhd', probs_low.astype(jnp.float32), value_part.astype(jnp.float32))
    mixed = mixed.reshape(slot_count, width).astype(jnp.bfloat16)
    hidden_one = tokens_wide + jnp.dot(mixed, w_proj, preferred_element_type=jnp.float32) + proj_bias.astype(jnp.float32)
    normed_mlp = layer_norm(hidden_one, mlp_gain.astype(jnp.float32), mlp_shift.astype(jnp.float32))
    act_mlp = normed_mlp.astype(jnp.bfloat16)
    pre_act = jnp.dot(act_mlp, w_up, preferred_element_type=jnp.float32) + up_bias.astype(jnp.float32)
    act_up = gelu_tanh(pre_act).astype(jnp.bfloat16)
    block_out = (hidden_one + jnp.dot(act_up, w_down, preferred_element_type=jnp.float32) + down_bias.astype(jnp.float32)) * live
    saved = (act_attn, qkv_full, log_total, mixed, hidden_one, act_mlp, pre_act, act_up)
    return (block_out.astype(jnp.bfloat16), saved)

def backward_pass(full, saved, tokens_blk, cotangent_blk, starts_blk, live):
    attn_gain, attn_shift, w_qkv, query_bias, value_bias, w_proj, proj_bias, mlp_gain, mlp_shift, w_up, up_bias, w_down, down_bias = full
    act_attn, qkv_full, log_total, mixed, hidden_one, act_mlp, pre_act, act_up = saved
    slot_count = tokens_blk.shape[0]
    width = tokens_blk.shape[1]
    tokens_wide = tokens_blk.astype(jnp.float32)
    grad_out = cotangent_blk.astype(jnp.float32) * live
    grad_low = grad_out.astype(jnp.bfloat16)
    g_down = jnp.dot(act_up.T, grad_low, preferred_element_type=jnp.float32)
    g_down_bias = lax.optimization_barrier(jnp.sum(grad_out, axis=0))
    grad_act = jnp.dot(grad_low, w_down.T, preferred_element_type=jnp.float32)
    gelu_value, gelu_back = jax.vjp(gelu_tanh, pre_act)
    grad_pre, = gelu_back(grad_act)
    grad_pre_low = grad_pre.astype(jnp.bfloat16)
    g_up = jnp.dot(act_mlp.T, grad_pre_low, preferred_element_type=jnp.float32)
    g_up_bias = lax.optimization_barrier(jnp.sum(grad_pre, axis=0))
    grad_normed = jnp.dot(grad_pre_low, w_up.T, preferred_element_type=jnp.float32)
    norm_value, norm_back = jax.vjp(layer_norm, hidden_one, mlp_gain.astype(jnp.float32), mlp_shift.astype(jnp.float32))
    grad_hidden_part, g_mlp_gain, g_mlp_shift = norm_back(grad_normed)
    grad_hidden = grad_out + grad_hidden_part
    grad_hidden_low = grad_hidden.astype(jnp.bfloat16)
    g_proj = jnp.dot(mixed.T, grad_hidden_low, preferred_element_type=jnp.float32)
    g_proj_bias = lax.optimization_barrier(jnp.sum(grad_hidden, axis=0))
    grad_mixed = jnp.dot(grad_hidden_low, w_proj.T, preferred_element_type=jnp.float32).astype(jnp.bfloat16)
    grad_mixed = grad_mixed.reshape(slot_count, width // HEAD_DIM, HEAD_DIM)
    query_part, key_part, value_part = split_heads(qkv_full, width)
    scores = score_block(query_part, key_part, starts_blk)
    attn_probs = jnp.exp(scores - log_total)
    probs_low = attn_probs.astype(jnp.bfloat16)
    grad_probs = jnp.einsum('qhd,khd->hqk', grad_mixed.astype(jnp.float32), value_part.astype(jnp.float32))
    grad_value = jnp.einsum('hqk,qhd->khd', probs_low.astype(jnp.float32), grad_mixed.astype(jnp.float32))
    row_dot = lax.optimization_barrier(jnp.sum(attn_probs * grad_probs, axis=-1, keepdims=True))
    grad_scores = (attn_probs * (grad_probs - row_dot) * HEAD_DIM ** (-0.5)).astype(jnp.bfloat16)
    grad_query = jnp.einsum('hqk,khd->qhd', grad_scores.astype(jnp.float32), key_part.astype(jnp.float32))
    grad_key = jnp.einsum('hqk,qhd->khd', grad_scores.astype(jnp.float32), query_part.astype(jnp.float32))
    grad_query = grad_query.reshape(slot_count, width)
    grad_key = grad_key.reshape(slot_count, width)
    grad_value = grad_value.reshape(slot_count, width)
    g_query_bias = lax.optimization_barrier(jnp.sum(grad_query, axis=0))
    g_value_bias = lax.optimization_barrier(jnp.sum(grad_value, axis=0))
    grad_qkv_low = jnp.concatenate([grad_query, grad_key, grad_value], axis=1).astype(jnp.bfloat16)
    g_qkv = jnp.dot(act_attn.T, grad_qkv_low, preferred_element_type=jnp.float32)
    grad_normed_attn = jnp.dot(grad_qkv_low, w_qkv.T, preferred_element_type=jnp.float32)
    first_value, first_back = jax.vjp(layer_norm, tokens_wide, attn_gain.astype(jnp.float32), attn_shift.astype(jnp.float32))
    grad_in_part, g_attn_gain, g_attn_shift = first_back(grad_normed_attn)
    grad_in = grad_hidden + grad_in_part
    grads = (g_attn_gain, g_attn_shift, g_qkv, g_query_bias, g_value_bias, g_proj, g_proj_bias, g_mlp_gain, g_mlp_shift, g_up, g_up_bias, g_down, g_down_bias)
    return (grad_in, grads)

def shaped(vector, length):
    return vector.reshape(N_SHARD, length // N_SHARD)

def reference(tokens, cotangent, starts, counts, attn_gain, attn_shift, w_qkv, query_bias, value_bias, w_proj, proj_bias, mlp_gain, mlp_shift, w_up, up_bias, w_down, down_bias):
    full = (attn_gain.reshape(D), attn_shift.reshape(D), w_qkv.reshape(D, 3 * D), query_bias.reshape(D), value_bias.reshape(D), w_proj, proj_bias.reshape(D), mlp_gain.reshape(D), mlp_shift.reshape(D), w_up, up_bias.reshape(FF), w_down, down_bias.reshape(D))
    block_count = N_FSDP * N_SHARD
    token_blocks = tokens.reshape(block_count, CAP, D)
    cotangent_blocks = cotangent.reshape(block_count, CAP, D)
    start_blocks = starts.reshape(block_count, CAP)

    def visit(running, pieces):
        tokens_blk, cotangent_blk, starts_blk, live_count = pieces
        live = (jnp.arange(CAP, dtype=jnp.int32) < live_count).astype(jnp.float32)[:, None]
        output_low, saved = forward_pass(full, tokens_blk, starts_blk, live)
        grad_in, grads = backward_pass(full, saved, tokens_blk, cotangent_blk, starts_blk, live)
        running = jax.tree.map(lambda total, extra: total + extra, running, grads)
        return (running, (output_low, grad_in))
    zeros_init = jax.tree.map(lambda tensor: jnp.zeros(tensor.shape, jnp.float32), full)
    totals, stacked = lax.scan(visit, zeros_init, (token_blocks, cotangent_blocks, start_blocks, counts))
    outputs_all, grads_all = stacked
    return (outputs_all.reshape(SLOTS, D), grads_all.reshape(SLOTS, D), shaped(totals[0], D), shaped(totals[1], D), totals[2].reshape(D, 3, D), shaped(totals[3], D), shaped(totals[4], D), totals[5], shaped(totals[6], D), shaped(totals[7], D), shaped(totals[8], D), totals[9], shaped(totals[10], FF), totals[11], shaped(totals[12], D))
```

```python
import jax
import jax.numpy as jnp
from jax import lax
from jax.sharding import PartitionSpec as P

HEAD_DIM = 64


NORM_EPS = 1e-05
NEG_FILL = -1e30


def gelu_tanh(values):
    return jax.nn.gelu(values, approximate=True)


def split_heads(qkv_full, quarter, slot_count):
    row_count = qkv_full.shape[0]
    grid = (row_count // slot_count, slot_count, quarter // HEAD_DIM, HEAD_DIM)
    query_part = qkv_full[:, :quarter].reshape(grid)
    key_part = qkv_full[:, quarter : 2 * quarter].reshape(grid)
    value_part = qkv_full[:, 2 * quarter :].reshape(grid)
    return (query_part, key_part, value_part)


def score_blocks(query_part, key_part, starts_grid):
    scores = jnp.einsum("bqhd,bkhd->bhqk", query_part, key_part, preferred_element_type=jnp.float32)
    scores = scores * HEAD_DIM ** (-0.5)
    positions = jnp.arange(scores.shape[2], dtype=jnp.int32)
    visible = (positions[None, None, :] >= starts_grid[:, :, None]) & (
        positions[None, None, :] <= positions[None, :, None]
    )
    return jnp.where(visible[:, None], scores, NEG_FILL)


def core(array):
    count = lax.axis_size("fsdp")
    return lax.ppermute(array, "fsdp", [(index, index ^ 1) for index in range(count)])


def pair(array):
    count = lax.axis_size("shard")
    return lax.ppermute(array, "shard", [(index, index ^ 1) for index in range(count)])


def far(array):
    count = lax.axis_size("shard")
    return lax.ppermute(array, "shard", [(index, index ^ 2) for index in range(count)])


def plane_groups():
    count = lax.axis_size("fsdp")
    return [[2 * step + bit for step in range(count // 2)] for bit in range(2)]


def gather_blocks(array):
    across = pair(array)
    return jnp.concatenate([array, core(array), across, core(across)], axis=0)


def return_blocks(partial):
    count = partial.shape[0] // 4
    sent = jnp.concatenate([partial[count : 2 * count], partial[3 * count :]]).astype(jnp.bfloat16)
    received = core(sent).astype(jnp.float32)
    across = (partial[2 * count : 3 * count] + received[count:]).astype(jnp.bfloat16)
    return (partial[:count] + received[:count]) + pair(across).astype(jnp.float32)


def by_bit(bit, mine, other, axis):
    return jnp.where(
        bit == 0,
        jnp.concatenate([mine, other], axis=axis),
        jnp.concatenate([other, mine], axis=axis),
    )


def to_rows(piece, bit):
    mine = lax.dynamic_index_in_dim(piece, bit, axis=1, keepdims=False)
    other = core(lax.dynamic_index_in_dim(piece, 1 - bit, axis=1, keepdims=False))
    return by_bit(bit, mine, other, 0)


def from_rows(rows, bit):
    split = rows.reshape(2, rows.shape[0] // 2, rows.shape[1])
    mine = lax.dynamic_index_in_dim(split, bit, axis=0, keepdims=False)
    other = core(lax.dynamic_index_in_dim(split, 1 - bit, axis=0, keepdims=False))
    return by_bit(bit, mine[:, None], other[:, None], 1)


def widen(rows, lengths):
    other = far(rows)
    parts = []
    at = 0
    for length in lengths:
        parts += [rows[:, at : at + length], other[:, at : at + length]]
        at += length
    return jnp.concatenate(parts, axis=1)


def narrow(rows, lengths):
    own, other = [], []
    at = 0
    for length in lengths:
        own.append(rows[:, at : at + length])
        other.append(rows[:, at + length : at + 2 * length])
        at += 2 * length
    received = far(jnp.concatenate(other, axis=1))
    total = jnp.concatenate(own, axis=1).astype(jnp.float32) + received.astype(jnp.float32)
    return total.astype(jnp.bfloat16)


def gather_plane(rows):
    return lax.all_gather(rows, "fsdp", axis=0, axis_index_groups=plane_groups(), tiled=True)


def reduce_plane(whole):
    return lax.psum_scatter(
        whole, "fsdp", scatter_dimension=0, axis_index_groups=plane_groups(), tiled=True
    )


def gather_vectors(vectors, starts):
    fsdp_count = lax.axis_size("fsdp")
    shard_count = lax.axis_size("shard")
    packed = jnp.concatenate([v.reshape(-1) for v in vectors] + [starts.astype(jnp.bfloat16)])
    spread_out = jnp.broadcast_to(packed, (fsdp_count * shard_count, packed.shape[0]))
    every = lax.all_to_all(spread_out, ("fsdp", "shard"), 0, 0, tiled=True)
    every = every.reshape(fsdp_count, shard_count, -1)
    full = []
    at = 0
    for v in vectors:
        piece = every[:, :, at : at + v.size]
        full.append(jnp.transpose(piece, (1, 0, 2)).reshape(shard_count, -1).astype(jnp.float32))
        at += v.size
    fsdp, shard = lax.axis_index("fsdp"), lax.axis_index("shard")
    rows = [
        lax.dynamic_slice(every, (fsdp ^ f, shard ^ s, at), (1, 1, starts.shape[0]))[0]
        for s in range(2)
        for f in range(2)
    ]
    return full, jnp.concatenate(rows, axis=0).astype(jnp.int32)


def own_part(vector, bits):
    high, low, bit = bits
    split = vector.reshape(2, 2, 2, -1)
    split = lax.dynamic_index_in_dim(split, low, axis=1, keepdims=False)
    split = lax.dynamic_index_in_dim(split, bit, axis=1, keepdims=False)
    return by_bit(high, split[0], split[1], 0)


def whole_part(part, bits):
    high, low, bit = bits
    split = part.reshape(2, 1, 1, -1)
    split = jnp.where(high == 0, split, split[::-1])
    place = jnp.arange(2)
    mask = (place[:, None] == low) & (place[None, :] == bit)
    return jnp.where(mask[None, :, :, None], split, 0.0).reshape(-1)


def reduce_vectors(wholes):
    fsdp_count = lax.axis_size("fsdp")
    shard_count = lax.axis_size("shard")
    parts = [w.reshape(shard_count, fsdp_count, -1) for w in wholes]
    packed = jnp.transpose(jnp.concatenate(parts, axis=2), (1, 0, 2))
    packed = packed.reshape(fsdp_count * shard_count, -1)
    received = lax.all_to_all(packed, ("fsdp", "shard"), 0, 0, tiled=True)
    total = jnp.sum(received, axis=0)
    out = []
    at = 0
    for p in parts:
        out.append(total[at : at + p.shape[2]].reshape(1, -1))
        at += p.shape[2]
    return out


def norm_parts(inputs):
    center = inputs - jnp.mean(inputs, axis=-1, keepdims=True)
    variance = jnp.mean(center * center, axis=-1, keepdims=True)
    scale = lax.rsqrt(variance + NORM_EPS)
    return center * scale, scale


def norm_back(unit, scale, gain, grad):
    grad_unit = grad * gain
    mean_grad = jnp.mean(grad_unit, axis=-1, keepdims=True)
    mean_dot = jnp.mean(grad_unit * unit, axis=-1, keepdims=True)
    return (
        scale * (grad_unit - mean_grad - unit * mean_dot),
        jnp.sum(grad * unit, axis=0),
        jnp.sum(grad, axis=0),
    )


def dot(left, right, left_dim, right_dim):
    return lax.dot_general(
        left, right, (((left_dim,), (right_dim,)), ((), ())), preferred_element_type=jnp.float32
    )


def on_device(
    tokens,
    cotangent,
    starts,
    counts,
    attn_gain,
    attn_shift,
    w_qkv,
    query_bias,
    value_bias,
    w_proj,
    proj_bias,
    mlp_gain,
    mlp_shift,
    w_up,
    up_bias,
    w_down,
    down_bias,
):
    bf16, f32 = jnp.bfloat16, jnp.float32
    slot_count, width = tokens.shape
    shard = lax.axis_index("shard")
    bits = (shard // 2, shard % 2, lax.axis_index("fsdp") % 2)
    bit = bits[2]
    rows = w_qkv.shape[0]
    quarter = w_qkv.shape[2]
    half = quarter // 2
    up_half = w_up.shape[1] // 2

    attn_piece = jnp.concatenate(
        [
            jnp.transpose(w_qkv.reshape(rows, 3, 2, half), (0, 2, 1, 3)).reshape(rows, 2, 3 * half),
            w_proj.T.reshape(rows, 2, half),
        ],
        axis=2,
    )
    attn_rows = widen(to_rows(attn_piece, bit), (half,) * 4)
    attn_full = gather_plane(attn_rows)
    w_qkv_full, w_proj_full = attn_full[:, : 3 * quarter], attn_full[:, 3 * quarter :]
    vectors, starts_grid = gather_vectors(
        (
            attn_gain,
            attn_shift,
            proj_bias,
            mlp_gain,
            mlp_shift,
            down_bias,
            query_bias,
            value_bias,
            up_bias,
        ),
        starts,
    )
    a_gain, a_shift, p_bias, m_gain, m_shift, d_bias = [v.reshape(-1) for v in vectors[:6]]
    q_bias, v_bias, u_bias = [own_part(v, bits) for v in vectors[6:]]
    mlp_piece = jnp.concatenate(
        [w_up.reshape(rows, 2, up_half), w_down.T.reshape(rows, 2, up_half)], axis=2
    )
    mlp_rows = widen(to_rows(mlp_piece, bit), (up_half,) * 2)
    w_up_full = gather_plane(mlp_rows[:, : 2 * up_half])
    w_down_full = gather_plane(mlp_rows[:, 2 * up_half :])

    live = (jnp.arange(slot_count, dtype=jnp.int32) < counts[0]).astype(f32)[:, None]
    grad_out = cotangent.astype(f32) * live
    tokens_wide = tokens.astype(f32)
    attn_unit, attn_scale = norm_parts(tokens_wide)
    act_rows = gather_blocks((attn_unit * a_gain + a_shift).astype(bf16))
    grad_low_rows = gather_blocks(grad_out.astype(bf16))
    row_count = act_rows.shape[0]
    qkv_bias = jnp.concatenate([q_bias, jnp.zeros_like(q_bias), v_bias])
    qkv_full = (dot(act_rows, w_qkv_full, 1, 0) + qkv_bias).astype(bf16)
    query_part, key_part, value_part = split_heads(qkv_full, quarter, slot_count)
    scores = score_blocks(query_part, key_part, starts_grid)
    row_max = jnp.max(scores, axis=-1, keepdims=True)
    log_total = row_max + jnp.log(jnp.sum(jnp.exp(scores - row_max), axis=-1, keepdims=True))
    probs = jnp.exp(scores - log_total)
    probs_low = probs.astype(bf16)
    mixed = jnp.einsum("bhqk,bkhd->bqhd", probs_low, value_part, preferred_element_type=f32)
    mixed = mixed.reshape(row_count, quarter).astype(bf16)
    attn_term = return_blocks(dot(mixed, w_proj_full, 1, 1))
    hidden_one = tokens_wide + attn_term + p_bias
    mlp_unit, mlp_scale = norm_parts(hidden_one)
    mlp_inputs = gather_blocks((mlp_unit * m_gain + m_shift).astype(bf16))
    pre_act = dot(mlp_inputs, w_up_full, 1, 0) + u_bias
    act_up, gelu_back = jax.vjp(gelu_tanh, pre_act)
    act_up = act_up.astype(bf16)
    grad_act = dot(grad_low_rows, w_down_full, 1, 0)
    (grad_pre,) = gelu_back(grad_act)
    grad_pre_low = grad_pre.astype(bf16)
    grad_normed = return_blocks(dot(grad_pre_low, w_up_full, 1, 1))
    g_down = dot(grad_low_rows, act_up, 0, 0).astype(bf16)
    g_up = dot(mlp_inputs, grad_pre_low, 0, 0).astype(bf16)
    g_up_bias = jnp.sum(grad_pre, axis=0)
    g_down_bias = jnp.sum(grad_out, axis=0)
    grad_hidden_part, g_mlp_gain, g_mlp_shift = norm_back(
        mlp_unit, mlp_scale, m_gain, grad_normed
    )
    grad_hidden = grad_out + grad_hidden_part
    grad_hidden, g_down, g_up = lax.optimization_barrier((grad_hidden, g_down, g_up))
    g_down = reduce_plane(g_down)
    g_up = reduce_plane(g_up)
    hidden_rows = gather_blocks(grad_hidden.astype(bf16))
    mlp_term = return_blocks(dot(act_up, w_down_full, 1, 1))
    block_out = (hidden_one + mlp_term + d_bias) * live
    g_proj_bias = jnp.sum(grad_hidden, axis=0)
    g_proj = dot(hidden_rows, mixed, 0, 0).astype(bf16)
    grad_mixed = dot(hidden_rows, w_proj_full, 1, 0).astype(bf16)
    grad_mixed = grad_mixed.reshape(
        row_count // slot_count, slot_count, quarter // HEAD_DIM, HEAD_DIM
    )
    grad_probs = jnp.einsum("bqhd,bkhd->bhqk", grad_mixed, value_part, preferred_element_type=f32)
    grad_value = jnp.einsum("bhqk,bqhd->bkhd", probs_low, grad_mixed, preferred_element_type=f32)
    row_dot = jnp.sum(probs * grad_probs, axis=-1, keepdims=True)
    grad_scores = (probs * (grad_probs - row_dot) * HEAD_DIM ** (-0.5)).astype(bf16)
    grad_query = jnp.einsum("bhqk,bkhd->bqhd", grad_scores, key_part, preferred_element_type=f32)
    grad_key = jnp.einsum("bhqk,bqhd->bkhd", grad_scores, query_part, preferred_element_type=f32)
    grad_query = grad_query.reshape(row_count, quarter)
    grad_key = grad_key.reshape(row_count, quarter)
    grad_value = grad_value.reshape(row_count, quarter)
    g_query_bias = jnp.sum(grad_query, axis=0)
    g_value_bias = jnp.sum(grad_value, axis=0)
    grad_qkv_low = jnp.concatenate([grad_query, grad_key, grad_value], axis=1).astype(bf16)
    g_qkv = dot(act_rows, grad_qkv_low, 0, 0).astype(bf16)
    g_attn = reduce_plane(jnp.concatenate([g_qkv, g_proj], axis=1))
    grad_normed_attn = return_blocks(dot(grad_qkv_low, w_qkv_full, 1, 1))
    grad_in_part, g_attn_gain, g_attn_shift = norm_back(
        attn_unit, attn_scale, a_gain, grad_normed_attn
    )
    grad_in = grad_hidden + grad_in_part
    small = reduce_vectors(
        (
            g_attn_gain,
            g_attn_shift,
            g_proj_bias,
            g_mlp_gain,
            g_mlp_shift,
            g_down_bias,
            whole_part(g_query_bias, bits),
            whole_part(g_value_bias, bits),
            whole_part(g_up_bias, bits),
        )
    )
    g_mlp = narrow(jnp.concatenate([g_up, g_down], axis=1), (up_half,) * 2)
    g_mlp = from_rows(g_mlp, bit).astype(f32)
    g_attn = from_rows(narrow(g_attn, (half,) * 4), bit).astype(f32)
    g_qkv = jnp.transpose(g_attn[:, :, : 3 * half].reshape(rows, 2, 3, half), (0, 2, 1, 3))
    return (
        block_out.astype(bf16),
        grad_in,
        small[0],
        small[1],
        g_qkv.reshape(w_qkv.shape),
        small[6],
        small[7],
        g_attn[:, :, 3 * half :].reshape(rows, quarter).T,
        small[2],
        small[3],
        small[4],
        g_mlp[:, :, :up_half].reshape(w_up.shape),
        small[8],
        g_mlp[:, :, up_half:].reshape(rows, 2 * up_half).T,
        small[5],
    )


def solution(mesh):
    in_specs = (
        P(("fsdp", "shard"), None),
        P(("fsdp", "shard"), None),
        P(("fsdp", "shard")),
        P(("fsdp", "shard")),
        P("shard", "fsdp"),
        P("shard", "fsdp"),
        P("fsdp", None, "shard"),
        P("shard", "fsdp"),
        P("shard", "fsdp"),
        P("shard", "fsdp"),
        P("shard", "fsdp"),
        P("shard", "fsdp"),
        P("shard", "fsdp"),
        P("fsdp", "shard"),
        P("shard", "fsdp"),
        P("shard", "fsdp"),
        P("shard", "fsdp"),
    )
    out_specs = (
        P(("fsdp", "shard"), None),
        P(("fsdp", "shard"), None),
        P("shard", "fsdp"),
        P("shard", "fsdp"),
        P("fsdp", None, "shard"),
        P("shard", "fsdp"),
        P("shard", "fsdp"),
        P("shard", "fsdp"),
        P("shard", "fsdp"),
        P("shard", "fsdp"),
        P("shard", "fsdp"),
        P("fsdp", "shard"),
        P("shard", "fsdp"),
        P("shard", "fsdp"),
        P("shard", "fsdp"),
    )
    return jax.shard_map(
        on_device, mesh=mesh, in_specs=in_specs, out_specs=out_specs, check_vma=False
    )
```

```python
import functools

import jax
import jax.numpy as jnp
from jax import lax
from jax.experimental import pallas as pl
from jax.experimental.pallas import tpu as pltpu
from jax.sharding import PartitionSpec as P

HEAD_DIM = 64
PLANE = 4
BLOCKS = 4
NORM_EPS = 1e-05
NEG_FILL = -1e30
GELU_ROOT = 0.7978845608028654
GELU_CUBE = 0.044715
F32, BF16 = jnp.float32, jnp.bfloat16


def core(array):
    count = lax.axis_size("fsdp")
    return lax.ppermute(array, "fsdp", [(index, index ^ 1) for index in range(count)])


def pair(array):
    count = lax.axis_size("shard")
    return lax.ppermute(array, "shard", [(index, index ^ 1) for index in range(count)])


def far(array):
    count = lax.axis_size("shard")
    return lax.ppermute(array, "shard", [(index, index ^ 2) for index in range(count)])


def by_bit(bit, mine, other, axis):
    return jnp.where(
        bit == 0,
        jnp.concatenate([mine, other], axis=axis),
        jnp.concatenate([other, mine], axis=axis),
    )


def to_rows(piece, bit):
    mine = lax.dynamic_index_in_dim(piece, bit, axis=1, keepdims=False)
    other = core(lax.dynamic_index_in_dim(piece, 1 - bit, axis=1, keepdims=False))
    return by_bit(bit, mine, other, 0)


def from_rows(rows, bit):
    split = rows.reshape(2, rows.shape[0] // 2, rows.shape[1])
    mine = lax.dynamic_index_in_dim(split, bit, axis=0, keepdims=False)
    other = core(lax.dynamic_index_in_dim(split, 1 - bit, axis=0, keepdims=False))
    return by_bit(bit, mine[:, None], other[:, None], 1)


def plane_count():
    return lax.axis_size("fsdp") // 2


def plane_index():
    return lax.axis_index("fsdp") // 2


def plane(array, distance):
    count = lax.axis_size("fsdp")
    return lax.ppermute(
        array, "fsdp", [(index, index ^ (2 * distance)) for index in range(count)]
    )


def ring(array, distance):
    count = lax.axis_size("shard")
    return lax.ppermute(array, "shard", [(index, index ^ distance) for index in range(count)])


def gather_ring(array):
    others = {k: ring(array, k) for k in (3, 2, 1)}
    return [array] + [others[k] for k in range(1, BLOCKS)]


def return_ring(own, *sent):
    others = {k: ring(sent[k - 1], k) for k in (3, 2, 1)}
    return [own] + [others[k] for k in range(1, BLOCKS)]


def plane_groups():
    return [[2 * step + bit for step in range(plane_count())] for bit in range(2)]


def reorder(array):
    if plane_count() != PLANE:
        return array
    size = array.shape[-1] // PLANE
    index = plane_index()
    for step in (1, 2):
        blocks = [array[..., j * size : (j + 1) * size] for j in range(PLANE)]
        swapped = jnp.concatenate([blocks[j ^ step] for j in range(PLANE)], axis=-1)
        array = jnp.where((index & step) != 0, swapped, array)
    return array


def gather_pieces(rows):
    if plane_count() == PLANE:
        return [rows] + [plane(rows, k) for k in range(1, PLANE)]
    whole = lax.all_gather(rows, "fsdp", axis=0, axis_index_groups=plane_groups(), tiled=True)
    size = whole.shape[0] // PLANE
    return [whole[k * size : (k + 1) * size] for k in range(PLANE)]


def reduce_plane(whole):
    if plane_count() == PLANE:
        size = whole.shape[0] // PLANE
        total = whole[:size].astype(F32)
        for k in range(1, PLANE):
            total = total + plane(whole[k * size : (k + 1) * size], k).astype(F32)
        return total
    return scatter_plane(whole).astype(F32)


def scatter_plane(whole):
    return lax.psum_scatter(
        whole, "fsdp", scatter_dimension=0, axis_index_groups=plane_groups(), tiled=True
    )


def hold(*values):
    return lax.optimization_barrier(values)


def gather_blocks(array):
    across = pair(array)
    return [array, core(array), across, core(across)]


def return_blocks(own, kept, sent):
    received = core(sent)
    count = own.shape[0]
    across = (kept + received[count:].astype(F32)).astype(BF16)
    return own, received, pair(across)


def pack_rows(*refs):
    out, rows = refs[-2:]
    rows[...] = jnp.zeros(rows.shape, rows.dtype)
    for row, ref in enumerate(refs[:-2]):
        rows[row : row + 1, : ref.shape[1]] = ref[...].astype(F32)
    out[...] = jnp.broadcast_to(rows[...].astype(out.dtype)[None], out.shape)


def run(kernel, outs, *operands, scratch=(), flops=0):
    spec = pl.BlockSpec(memory_space=pltpu.VMEM)
    moved = sum(o.size * o.dtype.itemsize for o in operands)
    moved += sum(functools.reduce(lambda a, b: a * b, shape) * 4 for shape, _ in outs)
    body = kernel.func if isinstance(kernel, functools.partial) else kernel
    return pl.pallas_call(
        kernel,
        out_shape=[jax.ShapeDtypeStruct(shape, kind) for shape, kind in outs],
        in_specs=[pl.BlockSpec(memory_space=pltpu.SMEM)] + [spec] * (len(operands) - 1),
        out_specs=[spec] * len(outs),
        scratch_shapes=list(scratch),
        cost_estimate=pl.CostEstimate(flops=flops, bytes_accessed=moved, transcendentals=0),
        name=body.__name__,
    )(*operands)


AT_PLANE, AT_SHARD, AT_FSDP, AT_COUNT = 0, 1, 2, 3


def mm(left, right, left_dim=1, right_dim=0):
    return lax.dot_general(
        left, right, (((left_dim,), (right_dim,)), ((), ())), preferred_element_type=F32
    )


def ordered(place, vec, row, swap):
    size = vec.shape[1] // PLANE
    blocks = []
    for j in range(PLANE):
        block = (place[AT_PLANE] ^ j) if swap else j
        blocks.append(vec[row : row + 1, pl.ds(pl.multiple_of(block * size, size), size)])
    return jnp.concatenate(blocks, axis=1)


def quarter_at(place, size, far_side):
    shard = place[AT_SHARD] ^ (2 if far_side else 0)
    return pl.multiple_of((shard * 2 + (place[AT_FSDP] & 1)) * size, size)


def unit_rows(values):
    center = values - jnp.mean(values, axis=-1, keepdims=True)
    scale = lax.rsqrt(jnp.mean(center * center, axis=-1, keepdims=True) + NORM_EPS)
    return center * scale, scale


def unit_back(unit, scale, grad_unit):
    mean_grad = jnp.mean(grad_unit, axis=-1, keepdims=True)
    mean_dot = jnp.mean(grad_unit * unit, axis=-1, keepdims=True)
    return scale * (grad_unit - mean_grad - unit * mean_dot)


def attn_forward(swap, place, vec, every, t0, t1, t2, t3, n0, n1, n2, n3, f0, f1, f2, f3,
                 act, qkv, probs, mixed, own, kept, sent):
    count = t0.shape[0]
    half = n0.shape[1] // 4
    width = vec.shape[1]
    size = width // PLANE
    gain, shift = ordered(place, vec, 0, swap), ordered(place, vec, 1, swap)
    for b, ref in enumerate((t0, t1, t2, t3)):
        unit, _ = unit_rows(ref[...].astype(F32))
        act[b * count : (b + 1) * count] = (unit * gain + shift).astype(BF16)
    for side, pieces in enumerate(((n0, n1, n2, n3), (f0, f1, f2, f3))):
        total = mm(act[:, :size], pieces[0][:, : 3 * half])
        for k in range(1, PLANE):
            total = total + mm(act[:, k * size : (k + 1) * size], pieces[k][:, : 3 * half])
        at = quarter_at(place, half, side == 1)
        bias = [vec[6:7, pl.ds(at, half)], jnp.zeros((1, half), F32), vec[7:8, pl.ds(at, half)]]
        total = total + jnp.concatenate(bias, axis=1)
        qkv[:, side * 3 * half : (side + 1) * 3 * half] = total.astype(BF16)
    keys = lax.broadcasted_iota(jnp.int32, (count, count), 0)
    queries = lax.broadcasted_iota(jnp.int32, (count, count), 1)

    def block(b, carry):
        rows = pl.ds(pl.multiple_of(b * count, count), count)
        device = (place[AT_FSDP] ^ (b & 1)) * place[AT_COUNT] + (place[AT_SHARD] ^ (b >> 1))
        starts = every[device].astype(F32)[9:10, :count].astype(jnp.int32)
        seen = (keys >= starts) & (keys <= queries)
        outs = []
        for h in range(BLOCKS):
            base = (h // 2) * 3 * half + (h % 2) * HEAD_DIM
            query = qkv[rows, base : base + HEAD_DIM]
            key = qkv[rows, base + half : base + half + HEAD_DIM]
            value = qkv[rows, base + 2 * half : base + 2 * half + HEAD_DIM]
            scores = jnp.where(seen, mm(key, query, 1, 1) * HEAD_DIM**-0.5, NEG_FILL)
            grown = jnp.exp(scores - jnp.max(scores, axis=0, keepdims=True))
            prob = grown / jnp.sum(grown, axis=0, keepdims=True)
            probs[b, h] = prob
            outs.append(mm(prob.astype(BF16), value, 0, 0))
        mixed[rows, :] = jnp.concatenate(outs, axis=1).astype(BF16)
        return carry

    lax.fori_loop(0, BLOCKS, block, 0)
    for k, (near, far_) in enumerate(zip((n0, n1, n2, n3), (f0, f1, f2, f3))):
        cols = slice(k * size, (k + 1) * size)
        part = mm(mixed[:, :half], near[:, 3 * half :], 1, 1)
        part = part + mm(mixed[:, half:], far_[:, 3 * half :], 1, 1)
        split_blocks(part, cols, count, own, kept, sent)


def split_blocks(part, cols, count, own, kept, sent):
    own[:, cols] = part[:count]
    kept[:, cols] = part[2 * count : 3 * count]
    sent[:count, cols] = part[count : 2 * count].astype(BF16)
    sent[count:, cols] = part[3 * count :].astype(BF16)


def natural(place, j, size, swap):
    return pl.ds(pl.multiple_of(((place[AT_PLANE] ^ j) if swap else j) * size, size), size)


def mlp_norm(swap, place, vec, tokens, own, received, across, hidden, hidden_natural, act):
    count, width = tokens.shape
    size = width // PLANE
    total = tokens[...].astype(F32) + ordered(place, vec, 2, swap)
    total = total + (own[...] + received[:count].astype(F32) + across[...].astype(F32))
    hidden[...] = total
    unit, _ = unit_rows(total)
    low = (unit * ordered(place, vec, 3, swap) + ordered(place, vec, 4, swap)).astype(BF16)
    for j in range(PLANE):
        there = natural(place, j, size, swap)
        act[:, there] = low[:, j * size : (j + 1) * size]
        hidden_natural[:, there] = total[:, j * size : (j + 1) * size]


def split_ring(part, cols, count, own, s1, s2, s3):
    own[:, cols] = part[:count]
    for k, ref in enumerate((s1, s2, s3)):
        ref[:, cols] = part[(k + 1) * count : (k + 2) * count].astype(BF16)


def mlp_forward(place, up_bias, up, down, a0, a1, a2, a3, g0, g1, g2, g3, act_up, grad_pre,
                bias_sum, own, s1, s2, s3, act, grad):
    count, width = a0.shape
    units = up.shape[1]
    tile = min(256, units)
    for b, (act_ref, grad_ref) in enumerate(zip((a0, a1, a2, a3), (g0, g1, g2, g3))):
        act[b * count : (b + 1) * count] = act_ref[...]
        grad[b * count : (b + 1) * count] = grad_ref[...]
    bias_sum[...] = jnp.zeros(bias_sum.shape, F32)
    start = place[AT_SHARD] * units

    def step(j, carry):
        inner = pl.ds(pl.multiple_of(j * tile, tile), tile)
        whole = pl.ds(pl.multiple_of(start + j * tile, tile), tile)
        pre = mm(act[...], up[:, inner]) + up_bias[:, whole]
        square = pre * pre
        bend = jnp.tanh(GELU_ROOT * (pre + GELU_CUBE * square * pre))
        half_in = 0.5 * (1.0 + bend)
        act_up[:, inner] = (pre * half_in).astype(BF16)
        slope = half_in + 0.5 * pre * (1.0 - bend * bend) * (
            GELU_ROOT * (1.0 + 3.0 * GELU_CUBE * square)
        )
        back = mm(grad[...], down[:, inner]) * slope
        grad_pre[:, inner] = back.astype(BF16)
        bias_sum[:, whole] = jnp.sum(back, axis=0, keepdims=True)
        return carry

    lax.fori_loop(0, units // tile, step, 0)
    size = width // PLANE
    for k in range(PLANE):
        cols = slice(k * size, (k + 1) * size)
        split_ring(mm(grad_pre[...], up[cols], 1, 1), cols, count, own, s1, s2, s3)


def unit_grads(swap, place, act_up, grad_pre, down, a0, a1, a2, a3, g0, g1, g2, g3,
               g_down, g_up, own, s1, s2, s3, rows):
    count, width = a0.shape
    half_units = g_up.shape[1] // 2
    size = width // PLANE
    for b, ref in enumerate((g0, g1, g2, g3)):
        rows[b * count : (b + 1) * count] = ref[...]
    for side in range(2):
        cols = slice(side * half_units, (side + 1) * half_units)
        g_down[:, cols] = mm(rows[...], act_up[:, cols], 0, 0).astype(BF16)
    for b, ref in enumerate((a0, a1, a2, a3)):
        rows[b * count : (b + 1) * count] = ref[...]
    if swap:
        size = width // (2 * PLANE)
        for far_core in range(2):
            for k in range(PLANE):
                block = (place[AT_FSDP] ^ (2 * k)) ^ far_core
                there = pl.ds(pl.multiple_of(block * size, size), size)
                at = (far_core * PLANE + k) * size
                g_up[at : at + size] = mm(rows[:, there], grad_pre[...], 0, 0).astype(BF16)
    else:
        for side in range(2):
            cols = slice(side * half_units, (side + 1) * half_units)
            g_up[:, cols] = mm(rows[...], grad_pre[:, cols], 0, 0).astype(BF16)
    size = width // PLANE
    for k in range(PLANE):
        cols = slice(k * size, (k + 1) * size)
        split_ring(mm(act_up[...], down[cols], 1, 1), cols, count, own, s1, s2, s3)


def norm_back(swap, place, vec, hidden, grad_out, own, r1, r2, r3, grad_hidden, low, sums):
    width = hidden.shape[1]
    size = width // PLANE
    unit, scale = unit_rows(hidden[...])
    blocks = []
    for j in range(PLANE):
        there = natural(place, j, size, swap)
        block = own[:, there]
        for ref in (r1, r2, r3):
            block = block + ref[:, there].astype(F32)
        blocks.append(block)
    grad = jnp.concatenate(blocks, axis=1)
    total = grad_out[...] + unit_back(unit, scale, grad * ordered(place, vec, 3, swap))
    grad_hidden[...] = total
    low[...] = total.astype(BF16)
    sums[0:1] = jnp.sum(grad * unit, axis=0, keepdims=True)
    sums[1:2] = jnp.sum(grad, axis=0, keepdims=True)
    sums[2:3] = jnp.sum(total, axis=0, keepdims=True)
    sums[3:4] = jnp.sum(grad_out[...], axis=0, keepdims=True)


def attn_backward(place, qkv, probs, mixed, act, h0, h1, h2, h3, n0, n1, n2, n3, f0, f1, f2, f3,
                  far_out, near_out, low, bias_sum, grad, grad_mixed):
    count, width = h0.shape
    size = width // PLANE
    half = n0.shape[1] // 4
    for b, ref in enumerate((h0, h1, h2, h3)):
        grad[b * count : (b + 1) * count] = ref[...]
    sides = ((n0, n1, n2, n3), (f0, f1, f2, f3))
    for side, pieces in enumerate(sides):
        total = mm(grad[:, :size], pieces[0][:, 3 * half :])
        for k in range(1, PLANE):
            total = total + mm(grad[:, k * size : (k + 1) * size], pieces[k][:, 3 * half :])
        grad_mixed[:, side * half : (side + 1) * half] = total.astype(BF16)
    bias_sum[...] = jnp.zeros(bias_sum.shape, F32)

    def block(b, sums):
        rows = pl.ds(pl.multiple_of(b * count, count), count)
        parts = [[], [], []]
        for h in range(BLOCKS):
            base = (h // 2) * 3 * half + (h % 2) * HEAD_DIM
            query = qkv[rows, base : base + HEAD_DIM]
            key = qkv[rows, base + half : base + half + HEAD_DIM]
            value = qkv[rows, base + 2 * half : base + 2 * half + HEAD_DIM]
            out = grad_mixed[rows, h * HEAD_DIM : (h + 1) * HEAD_DIM]
            prob = probs[b, h]
            back = mm(value, out, 1, 1)
            mean = jnp.sum(prob * back, axis=0, keepdims=True)
            scores = (prob * (back - mean) * HEAD_DIM**-0.5).astype(BF16)
            parts[0].append(mm(scores, key, 0, 0))
            parts[1].append(mm(scores, query, 1, 0))
            parts[2].append(mm(prob.astype(BF16), out, 1, 0))
        new = []
        for side in range(2):
            for which in range(3):
                joined = jnp.concatenate(parts[which][2 * side : 2 * side + 2], axis=1)
                base = (side * 3 + which) * half
                low[rows, base : base + half] = joined.astype(BF16)
                if which != 1:
                    new.append(jnp.sum(joined, axis=0, keepdims=True))
        return tuple(a + c for a, c in zip(sums, new))

    zero = jnp.zeros((1, half), F32)
    sums = lax.fori_loop(0, BLOCKS, block, (zero,) * 4)
    for side in range(2):
        at = quarter_at(place, half, side == 1)
        bias_sum[0:1, pl.ds(at, half)] = sums[2 * side]
        bias_sum[1:2, pl.ds(at, half)] = sums[2 * side + 1]
    for side, out in ((1, far_out), (0, near_out)):
        out[:, : 3 * half] = mm(
            act[...], low[:, side * 3 * half : (side + 1) * 3 * half], 0, 0
        ).astype(BF16)
        out[:, 3 * half :] = mm(
            grad[...], mixed[:, side * half : (side + 1) * half], 0, 0
        ).astype(BF16)


def attn_return(place, low, n0, n1, n2, n3, f0, f1, f2, f3, own, kept, sent):
    count = own.shape[0]
    half = n0.shape[1] // 4
    size = own.shape[1] // PLANE
    for k, (near, far_) in enumerate(zip((n0, n1, n2, n3), (f0, f1, f2, f3))):
        part = mm(low[:, : 3 * half], near[:, : 3 * half], 1, 1)
        part = part + mm(low[:, 3 * half :], far_[:, : 3 * half], 1, 1)
        split_blocks(part, slice(k * size, (k + 1) * size), count, own, kept, sent)


def input_back(swap, place, vec, tokens, grad_hidden, own, received, across, grad_in, sums):
    count = tokens.shape[0]
    unit, scale = unit_rows(tokens[...].astype(F32))
    grad = own[...] + received[:count].astype(F32) + across[...].astype(F32)
    gain = ordered(place, vec, 0, swap)
    grad_in[...] = grad_hidden[...] + unit_back(unit, scale, grad * gain)
    sums[0:1] = jnp.sum(grad * unit, axis=0, keepdims=True)
    sums[1:2] = jnp.sum(grad, axis=0, keepdims=True)


def on_device(
    tokens,
    cotangent,
    starts,
    counts,
    attn_gain,
    attn_shift,
    w_qkv,
    query_bias,
    value_bias,
    w_proj,
    proj_bias,
    mlp_gain,
    mlp_shift,
    w_up,
    up_bias,
    w_down,
    down_bias,
):
    slot_count, width = tokens.shape
    shard, fsdp = lax.axis_index("shard"), lax.axis_index("fsdp")
    shard_count, fsdp_count = lax.axis_size("shard"), lax.axis_size("fsdp")
    devices = shard_count * fsdp_count
    bit = fsdp % 2
    swap = plane_count() == PLANE
    place = jnp.stack([plane_index(), shard, fsdp, jnp.int32(shard_count)]).astype(jnp.int32)
    rows = w_qkv.shape[0]
    quarter = w_qkv.shape[2]
    half = quarter // 2
    units = w_up.shape[1]
    row_count = BLOCKS * slot_count

    with jax.named_scope("attn_weights"):
        attn_piece = jnp.concatenate(
            [
                jnp.transpose(w_qkv.reshape(rows, 3, 2, half), (0, 2, 1, 3)).reshape(
                    rows, 2, 3 * half
                ),
                w_proj.T.reshape(rows, 2, half),
            ],
            axis=2,
        )
        attn_near = to_rows(attn_piece, bit)
    with jax.named_scope("token_rows"):
        first, attn_near = hold(tokens, attn_near)
        token_low = reorder(first)
        token_across = pair(token_low)
    with jax.named_scope("attn_weights"):
        attn_far = far(attn_near)
        near = gather_pieces(attn_near)
    with jax.named_scope("vectors"):
        pieces = [
            v.reshape(1, -1)
            for v in (
                attn_gain,
                attn_shift,
                proj_bias,
                mlp_gain,
                mlp_shift,
                down_bias,
                query_bias,
                value_bias,
                up_bias,
                starts,
            )
        ]
        lanes = max(piece.shape[1] for piece in pieces)
        packed = pl.pallas_call(
            pack_rows,
            out_shape=jax.ShapeDtypeStruct((devices, 16, lanes), BF16),
            scratch_shapes=[pltpu.VMEM((16, lanes), F32)],
            name="pack_rows",
        )(*pieces)
    live = (jnp.arange(slot_count, dtype=jnp.int32) < counts[0]).astype(F32)[:, None]
    grad_natural = cotangent.astype(F32) * live
    grad_low = grad_natural.astype(BF16)
    grad_out = reorder(cotangent).astype(F32) * live
    grad_low, attn_far, token_low, token_across, packed, place, up, *near = hold(
        grad_low, attn_far, token_low, token_across, packed, place, w_up, *near
    )
    with jax.named_scope("mlp_weights"):
        up = lax.all_gather(up, "fsdp", axis=0, tiled=True)
    with jax.named_scope("attn_weights"):
        away = gather_pieces(attn_far)
    with jax.named_scope("token_rows"):
        token_rows = [token_low, core(token_low), token_across, core(token_across)]
    with jax.named_scope("vectors"):
        every = lax.all_to_all(packed, ("fsdp", "shard"), 0, 0, tiled=True)
        grid = every.reshape(fsdp_count, shard_count, 16, lanes)
        size = attn_gain.shape[1]
        vec = jnp.transpose(grid[:, :, :8, :size], (2, 1, 0, 3)).reshape(8, -1).astype(F32)
        size = up_bias.shape[1]
        up_vec = jnp.transpose(grid[:, :, 8, :size], (1, 0, 2)).reshape(1, -1).astype(F32)
    with jax.named_scope("grad_rows"):
        grad_rows = [grad_low, ring(grad_low, 1), ring(grad_low, 2), None]
    every, vec, up_vec, down, *held = hold(
        every, vec, up_vec, w_down.T, *grad_rows[:3], *token_rows, *away
    )
    grad_rows, token_rows, away = held[:3], held[3 : 3 + BLOCKS], held[3 + BLOCKS :]
    with jax.named_scope("mlp_weights"):
        down = lax.all_gather(down, "fsdp", axis=0, tiled=True)
    with jax.named_scope("grad_rows"):
        grad_rows.append(ring(grad_rows[0], 3))
    block = (slot_count, width)
    parts = [(block, F32), (block, F32), ((2 * slot_count, width), BF16)]
    act, qkv, probs, mixed, *attn_parts = run(
        functools.partial(attn_forward, swap),
        [
            ((row_count, width), BF16),
            ((row_count, 3 * quarter), BF16),
            ((BLOCKS, BLOCKS, slot_count, slot_count), F32),
            ((row_count, quarter), BF16),
            *parts,
        ],
        place,
        vec,
        every,
        *token_rows,
        *near,
        *away,
    )
    held = hold(*attn_parts, *grad_rows)
    attn_parts, grad_rows = held[:3], held[3:]
    with jax.named_scope("attn_return"):
        attn_term = return_blocks(*attn_parts)
    hidden, hidden_natural, mlp_act = run(
        functools.partial(mlp_norm, swap),
        [(block, F32), (block, F32), (block, BF16)],
        place,
        vec,
        token_low,
        *attn_term,
    )
    with jax.named_scope("mlp_inputs"):
        mlp_rows = gather_ring(mlp_act)
    whole = pltpu.VMEM((row_count, width), BF16)
    ring_parts = [(block, F32)] + [(block, BF16)] * (BLOCKS - 1)
    act_up, grad_pre, up_bias_sum, *normed_parts = run(
        mlp_forward,
        [((row_count, units), BF16), ((row_count, units), BF16), (up_vec.shape, F32), *ring_parts],
        place,
        up_vec,
        up,
        down,
        *mlp_rows,
        *grad_rows,
        scratch=[whole, whole],
    )
    with jax.named_scope("normed_return"):
        grad_normed = return_ring(*normed_parts)
    g_down, g_up, *mlp_parts = run(
        functools.partial(unit_grads, swap),
        [((width, units), BF16)] * 2 + ring_parts,
        place,
        act_up,
        grad_pre,
        down,
        *mlp_rows,
        *grad_rows,
        scratch=[whole],
    )
    with jax.named_scope("down_grads"):
        g_down_own = lax.psum_scatter(g_down, "fsdp", scatter_dimension=0, tiled=True)
    g_down, g_up, *held = hold(g_down, g_up, *mlp_parts, *grad_normed)
    mlp_parts, grad_normed = held[:BLOCKS], held[BLOCKS:]
    grad_hidden, hidden_low, sums = run(
        functools.partial(norm_back, swap),
        [(block, F32), (block, BF16), ((4, width), F32)],
        place,
        vec,
        hidden,
        grad_out,
        *grad_normed,
    )
    with jax.named_scope("hidden_rows"):
        hidden_rows = gather_blocks(hidden_low)
    with jax.named_scope("up_grads"):
        if swap:
            mid = width // 2
            g_up_half = (g_up[:mid].astype(F32) + core(g_up[mid:]).astype(F32)).astype(BF16)
        else:
            g_up_half = g_up
    g_up_half, *hidden_rows = hold(g_up_half, *hidden_rows)
    with jax.named_scope("mlp_return"):
        mlp_own, *mlp_others = return_ring(*mlp_parts)
    with jax.named_scope("up_grads"):
        if swap:
            g_up = reduce_plane(g_up_half)
        else:
            g_up = lax.psum_scatter(g_up, "fsdp", scatter_dimension=0, tiled=True).astype(F32)
    side = ((width, 4 * half), BF16)
    g_attn_far, g_attn_near, low, bias_sum = run(
        attn_backward,
        [side, side, ((row_count, 3 * quarter), BF16), ((2, width), F32)],
        place,
        qkv,
        probs,
        mixed,
        act,
        *hidden_rows,
        *near,
        *away,
        scratch=[whole, pltpu.VMEM((row_count, quarter), BF16)],
    )
    back_parts = run(attn_return, parts, place, low, *near, *away)
    g_attn_far, g_attn_near, g_up, *held = hold(
        g_attn_far, g_attn_near, g_up, *back_parts, *mlp_others[:2]
    )
    back_parts, mlp_others = held[:3], held[3:] + mlp_others[2:]
    with jax.named_scope("attn_grads"):
        g_attn_far = reduce_plane(g_attn_far).astype(BF16)
    with jax.named_scope("attn_back"):
        grad_attn = return_blocks(*back_parts)
    g_attn_far, g_attn_near, g_down_own, *held = hold(
        g_attn_far, g_attn_near, g_down_own, *grad_attn, *mlp_others
    )
    grad_attn, mlp_others = held[:3], held[3:]
    with jax.named_scope("attn_grads"):
        g_attn_near = reduce_plane(g_attn_near)
        g_attn_far = far(g_attn_far)
    with jax.named_scope("mlp_return"):
        mlp_term = mlp_own + sum(part.astype(F32) for part in mlp_others)
    block_out = ((hidden_natural + mlp_term + vec[5:6]) * live).astype(BF16)
    grad_in, in_sums = run(
        functools.partial(input_back, swap),
        [(block, F32), ((2, width), F32)],
        place,
        vec,
        token_low,
        grad_hidden,
        *grad_attn,
    )
    with jax.named_scope("small_grads"):
        flat = jnp.concatenate([reorder(jnp.concatenate([in_sums, sums], axis=0)), bias_sum])
        flat = flat.reshape(8, shard_count, fsdp_count, -1)
        flat = jnp.transpose(flat, (2, 1, 0, 3)).reshape(devices, -1)
        size = up_bias.shape[1]
        upper = jnp.transpose(up_bias_sum.reshape(shard_count, fsdp_count, size), (1, 0, 2))
        small = jnp.concatenate([flat, upper.reshape(devices, size)], axis=1)
        small, g_attn_near = hold(small, g_attn_near)
        small = jnp.sum(lax.all_to_all(small, ("fsdp", "shard"), 0, 0, tiled=True), axis=0)
        size = attn_gain.shape[1]
        g_vec = small[: 8 * size].reshape(8, 1, size)
        g_up_bias = small[8 * size :].reshape(1, -1)
    with jax.named_scope("attn_grads"):
        g_attn = from_rows((g_attn_near + g_attn_far.astype(F32)).astype(BF16), bit).astype(F32)
    g_qkv = jnp.transpose(g_attn[:, :, : 3 * half].reshape(rows, 2, 3, half), (0, 2, 1, 3))
    return (
        block_out,
        reorder(grad_in),
        g_vec[0],
        g_vec[1],
        g_qkv.reshape(w_qkv.shape),
        g_vec[6],
        g_vec[7],
        g_attn[:, :, 3 * half :].reshape(rows, quarter).T,
        g_vec[4],
        g_vec[2],
        g_vec[3],
        g_up,
        g_up_bias,
        g_down_own.astype(F32).T,
        g_vec[5],
    )


def solution(mesh):
    in_specs = (
        P(("fsdp", "shard"), None),
        P(("fsdp", "shard"), None),
        P(("fsdp", "shard")),
        P(("fsdp", "shard")),
        P("shard", "fsdp"),
        P("shard", "fsdp"),
        P("fsdp", None, "shard"),
        P("shard", "fsdp"),
        P("shard", "fsdp"),
        P("shard", "fsdp"),
        P("shard", "fsdp"),
        P("shard", "fsdp"),
        P("shard", "fsdp"),
        P("fsdp", "shard"),
        P("shard", "fsdp"),
        P("shard", "fsdp"),
        P("shard", "fsdp"),
    )
    out_specs = (
        P(("fsdp", "shard"), None),
        P(("fsdp", "shard"), None),
        P("shard", "fsdp"),
        P("shard", "fsdp"),
        P("fsdp", None, "shard"),
        P("shard", "fsdp"),
        P("shard", "fsdp"),
        P("shard", "fsdp"),
        P("shard", "fsdp"),
        P("shard", "fsdp"),
        P("shard", "fsdp"),
        P("fsdp", "shard"),
        P("shard", "fsdp"),
        P("shard", "fsdp"),
        P("shard", "fsdp"),
    )
    return jax.shard_map(
        on_device, mesh=mesh, in_specs=in_specs, out_specs=out_specs, check_vma=False
    )
```

```python
import functools

import jax
import jax.numpy as jnp
from jax import lax
from jax.experimental import pallas as pl
from jax.experimental.pallas import tpu as pltpu
from jax.sharding import PartitionSpec as P

HEAD_DIM = 64
PLANE = 4
BLOCKS = 4
NORM_EPS = 1e-05
NEG_FILL = -1e30
GELU_ROOT = 0.7978845608028654
GELU_CUBE = 0.044715
F32, BF16 = jnp.float32, jnp.bfloat16


def core(array):
    count = lax.axis_size("fsdp")
    return lax.ppermute(array, "fsdp", [(index, index ^ 1) for index in range(count)])


def pair(array):
    count = lax.axis_size("shard")
    return lax.ppermute(array, "shard", [(index, index ^ 1) for index in range(count)])


def far(array):
    count = lax.axis_size("shard")
    return lax.ppermute(array, "shard", [(index, index ^ 2) for index in range(count)])


def by_bit(bit, mine, other, axis):
    return jnp.where(
        bit == 0,
        jnp.concatenate([mine, other], axis=axis),
        jnp.concatenate([other, mine], axis=axis),
    )


def to_rows(piece, bit):
    mine = lax.dynamic_index_in_dim(piece, bit, axis=1, keepdims=False)
    other = core(lax.dynamic_index_in_dim(piece, 1 - bit, axis=1, keepdims=False))
    return by_bit(bit, mine, other, 0)


def from_rows(rows, bit):
    split = rows.reshape(2, rows.shape[0] // 2, rows.shape[1])
    mine = lax.dynamic_index_in_dim(split, bit, axis=0, keepdims=False)
    other = core(lax.dynamic_index_in_dim(split, 1 - bit, axis=0, keepdims=False))
    return by_bit(bit, mine[:, None], other[:, None], 1)


def plane_count():
    return lax.axis_size("fsdp") // 2


def plane_index():
    return lax.axis_index("fsdp") // 2


def plane(array, distance):
    count = lax.axis_size("fsdp")
    return lax.ppermute(
        array, "fsdp", [(index, index ^ (2 * distance)) for index in range(count)]
    )


def ring(array, distance):
    count = lax.axis_size("shard")
    return lax.ppermute(array, "shard", [(index, index ^ distance) for index in range(count)])


def gather_ring(array):
    others = {k: ring(array, k) for k in (3, 2, 1)}
    return [array] + [others[k] for k in range(1, BLOCKS)]


def return_ring(own, *sent):
    others = {k: ring(sent[k - 1], k) for k in (3, 2, 1)}
    return [own] + [others[k] for k in range(1, BLOCKS)]


def plane_groups():
    return [[2 * step + bit for step in range(plane_count())] for bit in range(2)]


def reorder(array):
    if plane_count() != PLANE:
        return array
    size = array.shape[-1] // PLANE
    index = plane_index()
    for step in (1, 2):
        blocks = [array[..., j * size : (j + 1) * size] for j in range(PLANE)]
        swapped = jnp.concatenate([blocks[j ^ step] for j in range(PLANE)], axis=-1)
        array = jnp.where((index & step) != 0, swapped, array)
    return array


def gather_pieces(rows):
    if plane_count() == PLANE:
        return [rows] + [plane(rows, k) for k in range(1, PLANE)]
    whole = lax.all_gather(rows, "fsdp", axis=0, axis_index_groups=plane_groups(), tiled=True)
    size = whole.shape[0] // PLANE
    return [whole[k * size : (k + 1) * size] for k in range(PLANE)]


def reduce_pieces(pieces):
    if plane_count() == PLANE:
        total = pieces[0].astype(F32)
        for k in range(1, PLANE):
            total = total + plane(pieces[k], k).astype(F32)
        return total
    return scatter_plane(jnp.concatenate(pieces, axis=0)).astype(F32)


def scatter_plane(whole):
    return lax.psum_scatter(
        whole, "fsdp", scatter_dimension=0, axis_index_groups=plane_groups(), tiled=True
    )


def hold(*values):
    return lax.optimization_barrier(values)


def gather_blocks(array):
    across = pair(array)
    return [array, core(array), across, core(across)]


def return_blocks(own, kept, sent):
    received = core(sent)
    count = own.shape[0]
    across = (kept + received[count:].astype(F32)).astype(BF16)
    return own, received, pair(across)


def pack_rows(*refs):
    out, rows = refs[-2:]
    rows[...] = jnp.zeros(rows.shape, rows.dtype)
    for row, ref in enumerate(refs[:-2]):
        rows[row : row + 1, : ref.shape[1]] = ref[...].astype(F32)
    out[...] = jnp.broadcast_to(rows[...].astype(out.dtype)[None], out.shape)


def run(kernel, outs, *operands, scratch=(), flops=0):
    spec = pl.BlockSpec(memory_space=pltpu.VMEM)
    moved = sum(o.size * o.dtype.itemsize for o in operands)
    moved += sum(functools.reduce(lambda a, b: a * b, shape) * 4 for shape, _ in outs)
    body = kernel.func if isinstance(kernel, functools.partial) else kernel
    return pl.pallas_call(
        kernel,
        out_shape=[jax.ShapeDtypeStruct(shape, kind) for shape, kind in outs],
        in_specs=[pl.BlockSpec(memory_space=pltpu.SMEM)] + [spec] * (len(operands) - 1),
        out_specs=[spec] * len(outs),
        scratch_shapes=list(scratch),
        cost_estimate=pl.CostEstimate(flops=flops, bytes_accessed=moved, transcendentals=0),
        name=body.__name__,
    )(*operands)


AT_PLANE, AT_SHARD, AT_FSDP, AT_COUNT = 0, 1, 2, 3


def mm(left, right, left_dim=1, right_dim=0):
    return lax.dot_general(
        left, right, (((left_dim,), (right_dim,)), ((), ())), preferred_element_type=F32
    )


def ordered(place, vec, row, swap):
    size = vec.shape[1] // PLANE
    blocks = []
    for j in range(PLANE):
        block = (place[AT_PLANE] ^ j) if swap else j
        blocks.append(vec[row : row + 1, pl.ds(pl.multiple_of(block * size, size), size)])
    return jnp.concatenate(blocks, axis=1)


def quarter_at(place, size, far_side):
    shard = place[AT_SHARD] ^ (2 if far_side else 0)
    return pl.multiple_of((shard * 2 + (place[AT_FSDP] & 1)) * size, size)


def unit_rows(values):
    center = values - jnp.mean(values, axis=-1, keepdims=True)
    scale = lax.rsqrt(jnp.mean(center * center, axis=-1, keepdims=True) + NORM_EPS)
    return center * scale, scale


def unit_back(unit, scale, grad_unit):
    mean_grad = jnp.mean(grad_unit, axis=-1, keepdims=True)
    mean_dot = jnp.mean(grad_unit * unit, axis=-1, keepdims=True)
    return scale * (grad_unit - mean_grad - unit * mean_dot)


def attn_forward(swap, place, vec, every, t0, t1, t2, t3, n0, n1, n2, n3, f0, f1, f2, f3,
                 act, qkv, probs, mixed, own, kept, sent):
    count = t0.shape[0]
    half = n0.shape[1] // 4
    width = vec.shape[1]
    size = width // PLANE
    gain, shift = ordered(place, vec, 0, swap), ordered(place, vec, 1, swap)
    for b, ref in enumerate((t0, t1, t2, t3)):
        unit, _ = unit_rows(ref[...].astype(F32))
        act[b * count : (b + 1) * count] = (unit * gain + shift).astype(BF16)
    for side, pieces in enumerate(((n0, n1, n2, n3), (f0, f1, f2, f3))):
        total = mm(act[:, :size], pieces[0][:, : 3 * half])
        for k in range(1, PLANE):
            total = total + mm(act[:, k * size : (k + 1) * size], pieces[k][:, : 3 * half])
        at = quarter_at(place, half, side == 1)
        bias = [vec[6:7, pl.ds(at, half)], jnp.zeros((1, half), F32), vec[7:8, pl.ds(at, half)]]
        total = total + jnp.concatenate(bias, axis=1)
        qkv[:, side * 3 * half : (side + 1) * 3 * half] = total.astype(BF16)
    keys = lax.broadcasted_iota(jnp.int32, (count, count), 0)
    queries = lax.broadcasted_iota(jnp.int32, (count, count), 1)

    def block(b, carry):
        rows = pl.ds(pl.multiple_of(b * count, count), count)
        device = (place[AT_FSDP] ^ (b & 1)) * place[AT_COUNT] + (place[AT_SHARD] ^ (b >> 1))
        starts = every[device].astype(F32)[9:10, :count].astype(jnp.int32)
        seen = (keys >= starts) & (keys <= queries)
        outs = []
        for h in range(BLOCKS):
            base = (h // 2) * 3 * half + (h % 2) * HEAD_DIM
            query = qkv[rows, base : base + HEAD_DIM]
            key = qkv[rows, base + half : base + half + HEAD_DIM]
            value = qkv[rows, base + 2 * half : base + 2 * half + HEAD_DIM]
            scores = jnp.where(seen, mm(key, query, 1, 1) * HEAD_DIM**-0.5, NEG_FILL)
            grown = jnp.exp(scores - jnp.max(scores, axis=0, keepdims=True))
            prob = grown / jnp.sum(grown, axis=0, keepdims=True)
            probs[b, h] = prob
            outs.append(mm(prob.astype(BF16), value, 0, 0))
        mixed[rows, :] = jnp.concatenate(outs, axis=1).astype(BF16)
        return carry

    lax.fori_loop(0, BLOCKS, block, 0, unroll=True)
    for k, (near, far_) in enumerate(zip((n0, n1, n2, n3), (f0, f1, f2, f3))):
        cols = slice(k * size, (k + 1) * size)
        part = mm(mixed[:, :half], near[:, 3 * half :], 1, 1)
        part = part + mm(mixed[:, half:], far_[:, 3 * half :], 1, 1)
        split_blocks(part, cols, count, own, kept, sent)


def split_blocks(part, cols, count, own, kept, sent):
    own[:, cols] = part[:count]
    kept[:, cols] = part[2 * count : 3 * count]
    sent[:count, cols] = part[count : 2 * count].astype(BF16)
    sent[count:, cols] = part[3 * count :].astype(BF16)


def natural(place, j, size, swap):
    return pl.ds(pl.multiple_of(((place[AT_PLANE] ^ j) if swap else j) * size, size), size)


def mlp_norm(swap, place, vec, tokens, own, received, across, hidden, hidden_natural, act):
    count, width = tokens.shape
    size = width // PLANE
    total = tokens[...].astype(F32) + ordered(place, vec, 2, swap)
    total = total + (own[...] + received[:count].astype(F32) + across[...].astype(F32))
    hidden[...] = total
    unit, _ = unit_rows(total)
    low = (unit * ordered(place, vec, 3, swap) + ordered(place, vec, 4, swap)).astype(BF16)
    for j in range(PLANE):
        there = natural(place, j, size, swap)
        act[:, there] = low[:, j * size : (j + 1) * size]
        hidden_natural[:, there] = total[:, j * size : (j + 1) * size]


def split_ring(part, cols, count, own, s1, s2, s3):
    own[:, cols] = part[:count]
    for k, ref in enumerate((s1, s2, s3)):
        ref[:, cols] = part[(k + 1) * count : (k + 2) * count].astype(BF16)


def shard_block(place, ref, distance, count):
    return ref[pl.ds(pl.multiple_of((place[AT_SHARD] ^ distance) * count, count), count)]


def mlp_forward(place, up_bias, both, a0, a1, a2, a3, grads, act_up, grad_pre,
                bias_sum, own, s1, s2, s3, act, grad):
    count, width = a0.shape
    units = both.shape[1] // 2
    tile = min(256, units)
    for b, act_ref in enumerate((a0, a1, a2, a3)):
        act[b * count : (b + 1) * count] = act_ref[...]
        grad[b * count : (b + 1) * count] = shard_block(place, grads, b, count)
    bias_sum[...] = jnp.zeros(bias_sum.shape, F32)
    start = place[AT_SHARD] * units

    def step(j, carry):
        inner = pl.ds(pl.multiple_of(j * tile, tile), tile)
        whole = pl.ds(pl.multiple_of(start + j * tile, tile), tile)
        second = pl.ds(pl.multiple_of(units + j * tile, tile), tile)
        pre = mm(act[...], both[:, inner]) + up_bias[:, whole]
        square = pre * pre
        bend = jnp.tanh(GELU_ROOT * (pre + GELU_CUBE * square * pre))
        half_in = 0.5 * (1.0 + bend)
        act_up[:, inner] = (pre * half_in).astype(BF16)
        slope = half_in + 0.5 * pre * (1.0 - bend * bend) * (
            GELU_ROOT * (1.0 + 3.0 * GELU_CUBE * square)
        )
        back = mm(grad[...], both[:, second]) * slope
        grad_pre[:, inner] = back.astype(BF16)
        bias_sum[:, whole] = jnp.sum(back, axis=0, keepdims=True)
        return carry

    lax.fori_loop(0, units // tile, step, 0)
    size = width // PLANE
    for k in range(PLANE):
        cols = slice(k * size, (k + 1) * size)
        split_ring(mm(grad_pre[...], both[cols, :units], 1, 1), cols, count, own, s1, s2, s3)


def unit_grads(swap, place, act_up, grad_pre, both, a0, a1, a2, a3, grads,
               g_down, g_up, g_up_sent, own, s1, s2, s3, rows):
    count, width = a0.shape
    half_units = g_up.shape[1] // 2
    size = width // PLANE
    for b in range(BLOCKS):
        rows[b * count : (b + 1) * count] = shard_block(place, grads, b, count)
    for side in range(2):
        cols = slice(side * half_units, (side + 1) * half_units)
        g_down[:, cols] = mm(rows[...], act_up[:, cols], 0, 0).astype(BF16)
    for b, ref in enumerate((a0, a1, a2, a3)):
        rows[b * count : (b + 1) * count] = ref[...]
    if swap:
        size = width // (2 * PLANE)
        for far_core in range(2):
            for k in range(PLANE):
                block = (place[AT_FSDP] ^ (2 * k)) ^ far_core
                there = pl.ds(pl.multiple_of(block * size, size), size)
                part = mm(rows[:, there], grad_pre[...], 0, 0).astype(BF16)
                (g_up_sent if far_core else g_up)[k * size : (k + 1) * size] = part
    else:
        for side, out in enumerate((g_up, g_up_sent)):
            cols = slice(side * width // 2, (side + 1) * width // 2)
            out[...] = mm(rows[:, cols], grad_pre[...], 0, 0).astype(BF16)
    size = width // PLANE
    for k in range(PLANE):
        cols = slice(k * size, (k + 1) * size)
        split_ring(mm(act_up[...], both[cols, act_up.shape[1] :], 1, 1), cols, count, own, s1, s2, s3)


def norm_back(swap, place, vec, hidden, grad_out, own, r1, r2, r3, grad_hidden, low, sums):
    width = hidden.shape[1]
    size = width // PLANE
    unit, scale = unit_rows(hidden[...])
    blocks = []
    for j in range(PLANE):
        there = natural(place, j, size, swap)
        block = own[:, there]
        for ref in (r1, r2, r3):
            block = block + ref[:, there].astype(F32)
        blocks.append(block)
    grad = jnp.concatenate(blocks, axis=1)
    total = grad_out[...] + unit_back(unit, scale, grad * ordered(place, vec, 3, swap))
    grad_hidden[...] = total
    low[...] = total.astype(BF16)
    sums[0:1] = jnp.sum(grad * unit, axis=0, keepdims=True)
    sums[1:2] = jnp.sum(grad, axis=0, keepdims=True)
    sums[2:3] = jnp.sum(total, axis=0, keepdims=True)
    sums[3:4] = jnp.sum(grad_out[...], axis=0, keepdims=True)


def attn_backward(place, qkv, probs, mixed, act, h0, h1, h2, h3, n0, n1, n2, n3, f0, f1, f2, f3,
                  far0, far1, far2, far3, near0, near1, near2, near3, low, bias_sum, grad,
                  grad_mixed):
    count, width = h0.shape
    size = width // PLANE
    half = n0.shape[1] // 4
    for b, ref in enumerate((h0, h1, h2, h3)):
        grad[b * count : (b + 1) * count] = ref[...]
    sides = ((n0, n1, n2, n3), (f0, f1, f2, f3))
    for side, pieces in enumerate(sides):
        total = mm(grad[:, :size], pieces[0][:, 3 * half :])
        for k in range(1, PLANE):
            total = total + mm(grad[:, k * size : (k + 1) * size], pieces[k][:, 3 * half :])
        grad_mixed[:, side * half : (side + 1) * half] = total.astype(BF16)
    bias_sum[...] = jnp.zeros(bias_sum.shape, F32)

    def block(b, sums):
        rows = pl.ds(pl.multiple_of(b * count, count), count)
        parts = [[], [], []]
        for h in range(BLOCKS):
            base = (h // 2) * 3 * half + (h % 2) * HEAD_DIM
            query = qkv[rows, base : base + HEAD_DIM]
            key = qkv[rows, base + half : base + half + HEAD_DIM]
            value = qkv[rows, base + 2 * half : base + 2 * half + HEAD_DIM]
            out = grad_mixed[rows, h * HEAD_DIM : (h + 1) * HEAD_DIM]
            prob = probs[b, h]
            back = mm(value, out, 1, 1)
            mean = jnp.sum(prob * back, axis=0, keepdims=True)
            scores = (prob * (back - mean) * HEAD_DIM**-0.5).astype(BF16)
            parts[0].append(mm(scores, key, 0, 0))
            parts[1].append(mm(scores, query, 1, 0))
            parts[2].append(mm(prob.astype(BF16), out, 1, 0))
        new = []
        for side in range(2):
            for which in range(3):
                joined = jnp.concatenate(parts[which][2 * side : 2 * side + 2], axis=1)
                base = (side * 3 + which) * half
                low[rows, base : base + half] = joined.astype(BF16)
                if which != 1:
                    new.append(jnp.sum(joined, axis=0, keepdims=True))
        return tuple(a + c for a, c in zip(sums, new))

    zero = jnp.zeros((1, half), F32)
    sums = lax.fori_loop(0, BLOCKS, block, (zero,) * 4, unroll=True)
    for side in range(2):
        at = quarter_at(place, half, side == 1)
        bias_sum[0:1, pl.ds(at, half)] = sums[2 * side]
        bias_sum[1:2, pl.ds(at, half)] = sums[2 * side + 1]
    for side, outs in ((1, (far0, far1, far2, far3)), (0, (near0, near1, near2, near3))):
        for k, out in enumerate(outs):
            cols = slice(k * size, (k + 1) * size)
            out[:, : 3 * half] = mm(
                act[:, cols], low[:, side * 3 * half : (side + 1) * 3 * half], 0, 0
            ).astype(BF16)
            out[:, 3 * half :] = mm(
                grad[:, cols], mixed[:, side * half : (side + 1) * half], 0, 0
            ).astype(BF16)


def attn_return(place, low, n0, n1, n2, n3, f0, f1, f2, f3, own, kept, sent):
    count = own.shape[0]
    half = n0.shape[1] // 4
    size = own.shape[1] // PLANE
    for k, (near, far_) in enumerate(zip((n0, n1, n2, n3), (f0, f1, f2, f3))):
        part = mm(low[:, : 3 * half], near[:, : 3 * half], 1, 1)
        part = part + mm(low[:, 3 * half :], far_[:, : 3 * half], 1, 1)
        split_blocks(part, slice(k * size, (k + 1) * size), count, own, kept, sent)


def input_back(swap, place, vec, tokens, grad_hidden, own, received, across, grad_in, sums):
    count = tokens.shape[0]
    unit, scale = unit_rows(tokens[...].astype(F32))
    grad = own[...] + received[:count].astype(F32) + across[...].astype(F32)
    gain = ordered(place, vec, 0, swap)
    grad_in[...] = grad_hidden[...] + unit_back(unit, scale, grad * gain)
    sums[0:1] = jnp.sum(grad * unit, axis=0, keepdims=True)
    sums[1:2] = jnp.sum(grad, axis=0, keepdims=True)


def on_device(
    tokens,
    cotangent,
    starts,
    counts,
    attn_gain,
    attn_shift,
    w_qkv,
    query_bias,
    value_bias,
    w_proj,
    proj_bias,
    mlp_gain,
    mlp_shift,
    w_up,
    up_bias,
    w_down,
    down_bias,
):
    slot_count, width = tokens.shape
    shard, fsdp = lax.axis_index("shard"), lax.axis_index("fsdp")
    shard_count, fsdp_count = lax.axis_size("shard"), lax.axis_size("fsdp")
    devices = shard_count * fsdp_count
    bit = fsdp % 2
    swap = plane_count() == PLANE
    place = jnp.stack([plane_index(), shard, fsdp, jnp.int32(shard_count)]).astype(jnp.int32)
    rows = w_qkv.shape[0]
    quarter = w_qkv.shape[2]
    half = quarter // 2
    units = w_up.shape[1]
    row_count = BLOCKS * slot_count

    with jax.named_scope("attn_weights"):
        attn_piece = jnp.concatenate(
            [
                jnp.transpose(w_qkv.reshape(rows, 3, 2, half), (0, 2, 1, 3)).reshape(
                    rows, 2, 3 * half
                ),
                w_proj.T.reshape(rows, 2, half),
            ],
            axis=2,
        )
        attn_near = to_rows(attn_piece, bit)
    with jax.named_scope("token_rows"):
        first, attn_near = hold(tokens, attn_near)
        token_low = reorder(first)
        token_across = pair(token_low)
    with jax.named_scope("attn_weights"):
        attn_far = far(attn_near)
        near = gather_pieces(attn_near)
    with jax.named_scope("vectors"):
        pieces = [
            v.reshape(1, -1)
            for v in (
                attn_gain,
                attn_shift,
                proj_bias,
                mlp_gain,
                mlp_shift,
                down_bias,
                query_bias,
                value_bias,
                up_bias,
                starts,
            )
        ]
        lanes = max(piece.shape[1] for piece in pieces)
        packed = pl.pallas_call(
            pack_rows,
            out_shape=jax.ShapeDtypeStruct((devices, 16, lanes), BF16),
            scratch_shapes=[pltpu.VMEM((16, lanes), F32)],
            name="pack_rows",
        )(*pieces)
    live = (jnp.arange(slot_count, dtype=jnp.int32) < counts[0]).astype(F32)[:, None]
    grad_natural = cotangent.astype(F32) * live
    grad_low = grad_natural.astype(BF16)
    grad_out = reorder(cotangent).astype(F32) * live
    mlp_piece = jnp.concatenate([w_up, w_down.T], axis=1)
    grad_low, attn_far, token_low, token_across, packed, place, mlp_piece, *near = hold(
        grad_low, attn_far, token_low, token_across, packed, place, mlp_piece, *near
    )
    with jax.named_scope("grad_rows"):
        grad_rows = lax.all_gather(grad_low, "shard", axis=0, tiled=True)
    with jax.named_scope("attn_weights"):
        away = gather_pieces(attn_far)
    with jax.named_scope("token_rows"):
        token_rows = [token_low, core(token_low), token_across, core(token_across)]
    with jax.named_scope("vectors"):
        every = lax.all_to_all(packed, ("fsdp", "shard"), 0, 0, tiled=True)
        grid = every.reshape(fsdp_count, shard_count, 16, lanes)
        size = attn_gain.shape[1]
        vec = jnp.transpose(grid[:, :, :8, :size], (2, 1, 0, 3)).reshape(8, -1).astype(F32)
        size = up_bias.shape[1]
        up_vec = jnp.transpose(grid[:, :, 8, :size], (1, 0, 2)).reshape(1, -1).astype(F32)
    every, vec, up_vec, mlp_piece, *held = hold(
        every, vec, up_vec, mlp_piece, *token_rows, *away
    )
    token_rows, away = held[:BLOCKS], held[BLOCKS:]
    with jax.named_scope("mlp_weights"):
        both = lax.all_gather(mlp_piece, "fsdp", axis=0, tiled=True)
    block = (slot_count, width)
    parts = [(block, F32), (block, F32), ((2 * slot_count, width), BF16)]
    act, qkv, probs, mixed, *attn_parts = run(
        functools.partial(attn_forward, swap),
        [
            ((row_count, width), BF16),
            ((row_count, 3 * quarter), BF16),
            ((BLOCKS, BLOCKS, slot_count, slot_count), F32),
            ((row_count, quarter), BF16),
            *parts,
        ],
        place,
        vec,
        every,
        *token_rows,
        *near,
        *away,
    )
    with jax.named_scope("attn_return"):
        attn_term = return_blocks(*attn_parts)
    hidden, hidden_natural, mlp_act = run(
        functools.partial(mlp_norm, swap),
        [(block, F32), (block, F32), (block, BF16)],
        place,
        vec,
        token_low,
        *attn_term,
    )
    with jax.named_scope("mlp_inputs"):
        mlp_rows = gather_ring(mlp_act)
    whole = pltpu.VMEM((row_count, width), BF16)
    ring_parts = [(block, F32)] + [(block, BF16)] * (BLOCKS - 1)
    act_up, grad_pre, up_bias_sum, *normed_parts = run(
        mlp_forward,
        [((row_count, units), BF16), ((row_count, units), BF16), (up_vec.shape, F32), *ring_parts],
        place,
        up_vec,
        both,
        *mlp_rows,
        grad_rows,
        scratch=[whole, whole],
    )
    with jax.named_scope("normed_return"):
        grad_normed = return_ring(*normed_parts)
    half_rows = ((width // 2, units), BF16)
    g_down, g_up, g_up_sent, *mlp_parts = run(
        functools.partial(unit_grads, swap),
        [((width, units), BF16), half_rows, half_rows, *ring_parts],
        place,
        act_up,
        grad_pre,
        both,
        *mlp_rows,
        grad_rows,
        scratch=[whole],
    )
    with jax.named_scope("down_grads"):
        g_down_own = lax.psum_scatter(g_down, "fsdp", scatter_dimension=0, tiled=True)
    g_down, g_up, g_up_sent, *held = hold(g_down, g_up, g_up_sent, *mlp_parts, *grad_normed)
    mlp_parts, grad_normed = held[:BLOCKS], held[BLOCKS:]
    grad_hidden, hidden_low, sums = run(
        functools.partial(norm_back, swap),
        [(block, F32), (block, BF16), ((4, width), F32)],
        place,
        vec,
        hidden,
        grad_out,
        *grad_normed,
    )
    with jax.named_scope("up_grads"):
        if swap:
            g_up_half = (g_up.astype(F32) + core(g_up_sent).astype(F32)).astype(BF16)
        else:
            g_up_half = jnp.concatenate([g_up, g_up_sent], axis=0)
    with jax.named_scope("hidden_rows"):
        across, g_up_half = hold(pair(hidden_low), g_up_half)
        hidden_rows = [hidden_low, core(hidden_low), across, core(across)]
    with jax.named_scope("up_grads"):
        if swap:
            g_up_parts = [g_up_half[k * rows : (k + 1) * rows] for k in range(PLANE)]
            g_up_parts = g_up_parts[:1] + [plane(g_up_parts[k], k) for k in range(1, PLANE)]
        else:
            g_up_parts = [lax.psum_scatter(g_up_half, "fsdp", scatter_dimension=0, tiled=True)]
    with jax.named_scope("mlp_return"):
        mlp_own, *mlp_others = return_ring(*mlp_parts)
    side = ((width // PLANE, 4 * half), BF16)
    *held, low, bias_sum = run(
        attn_backward,
        [side] * (2 * PLANE) + [((row_count, 3 * quarter), BF16), ((2, width), F32)],
        place,
        qkv,
        probs,
        mixed,
        act,
        *hidden_rows,
        *near,
        *away,
        scratch=[whole, pltpu.VMEM((row_count, quarter), BF16)],
    )
    g_attn_far, g_attn_near = held[:PLANE], held[PLANE:]
    back_parts = run(attn_return, parts, place, low, *near, *away)
    m1, m2, *held = hold(
        *mlp_others[:2], *back_parts, *g_up_parts, *g_attn_far, *g_attn_near
    )
    mlp_others = [m1, m2, *mlp_others[2:]]
    back_parts, g_up_parts, held = held[:3], held[3 : -2 * PLANE], held[-2 * PLANE :]
    g_attn_far, g_attn_near = held[:PLANE], held[PLANE:]
    with jax.named_scope("attn_grads"):
        g_attn_far = reduce_pieces(g_attn_far).astype(BF16)
    with jax.named_scope("attn_back"):
        grad_attn = return_blocks(*back_parts)
    g_attn_far, g_down_own, *held = hold(
        g_attn_far, g_down_own, *g_attn_near, *grad_attn, *mlp_others
    )
    g_attn_near, held = held[:PLANE], held[PLANE:]
    grad_attn, mlp_others = held[:3], held[3:]
    with jax.named_scope("up_grads"):
        g_up = sum(part.astype(F32) for part in g_up_parts)
    with jax.named_scope("attn_grads"):
        if swap:
            near_parts = g_attn_near[:1] + [plane(g_attn_near[k], k) for k in range(1, PLANE)]
        else:
            near_parts = [scatter_plane(jnp.concatenate(g_attn_near, axis=0))]
        g_attn_far = far(g_attn_far)
    with jax.named_scope("mlp_return"):
        mlp_term = mlp_own + sum(part.astype(F32) for part in mlp_others)
    block_out = ((hidden_natural + mlp_term + vec[5:6]) * live).astype(BF16)
    grad_in, in_sums = run(
        functools.partial(input_back, swap),
        [(block, F32), ((2, width), F32)],
        place,
        vec,
        token_low,
        grad_hidden,
        *grad_attn,
    )
    with jax.named_scope("small_grads"):
        flat = jnp.concatenate([reorder(jnp.concatenate([in_sums, sums], axis=0)), bias_sum])
        flat = flat.reshape(8, shard_count, fsdp_count, -1)
        flat = jnp.transpose(flat, (2, 1, 0, 3)).reshape(devices, -1)
        size = up_bias.shape[1]
        upper = jnp.transpose(up_bias_sum.reshape(shard_count, fsdp_count, size), (1, 0, 2))
        small = jnp.concatenate([flat, upper.reshape(devices, size)], axis=1)
        small, near_parts[-1] = hold(small, near_parts[-1])
        small = jnp.sum(lax.all_to_all(small, ("fsdp", "shard"), 0, 0, tiled=True), axis=0)
        size = attn_gain.shape[1]
        g_vec = small[: 8 * size].reshape(8, 1, size)
        g_up_bias = small[8 * size :].reshape(1, -1)
    with jax.named_scope("attn_grads"):
        g_attn_near = sum(part.astype(F32) for part in near_parts)
        g_attn = from_rows((g_attn_near + g_attn_far.astype(F32)).astype(BF16), bit).astype(F32)
    g_qkv = jnp.transpose(g_attn[:, :, : 3 * half].reshape(rows, 2, 3, half), (0, 2, 1, 3))
    return (
        block_out,
        reorder(grad_in),
        g_vec[0],
        g_vec[1],
        g_qkv.reshape(w_qkv.shape),
        g_vec[6],
        g_vec[7],
        g_attn[:, :, 3 * half :].reshape(rows, quarter).T,
        g_vec[4],
        g_vec[2],
        g_vec[3],
        g_up,
        g_up_bias,
        g_down_own.astype(F32).T,
        g_vec[5],
    )


def solution(mesh):
    in_specs = (
        P(("fsdp", "shard"), None),
        P(("fsdp", "shard"), None),
        P(("fsdp", "shard")),
        P(("fsdp", "shard")),
        P("shard", "fsdp"),
        P("shard", "fsdp"),
        P("fsdp", None, "shard"),
        P("shard", "fsdp"),
        P("shard", "fsdp"),
        P("shard", "fsdp"),
        P("shard", "fsdp"),
        P("shard", "fsdp"),
        P("shard", "fsdp"),
        P("fsdp", "shard"),
        P("shard", "fsdp"),
        P("shard", "fsdp"),
        P("shard", "fsdp"),
    )
    out_specs = (
        P(("fsdp", "shard"), None),
        P(("fsdp", "shard"), None),
        P("shard", "fsdp"),
        P("shard", "fsdp"),
        P("fsdp", None, "shard"),
        P("shard", "fsdp"),
        P("shard", "fsdp"),
        P("shard", "fsdp"),
        P("shard", "fsdp"),
        P("shard", "fsdp"),
        P("shard", "fsdp"),
        P("fsdp", "shard"),
        P("shard", "fsdp"),
        P("shard", "fsdp"),
        P("shard", "fsdp"),
    )
    return jax.shard_map(
        on_device, mesh=mesh, in_specs=in_specs, out_specs=out_specs, check_vma=False
    )
```

```python
import functools

import jax
import jax.numpy as jnp
from jax import lax
from jax.experimental import pallas as pl
from jax.experimental.pallas import tpu as pltpu
from jax.sharding import PartitionSpec as P

HEAD_DIM = 64
PLANE = 4
BLOCKS = 4
NORM_EPS = 1e-05
NEG_FILL = -1e30
GELU_ROOT = 0.7978845608028654
GELU_CUBE = 0.044715
F32, BF16 = jnp.float32, jnp.bfloat16


def core(array):
    count = lax.axis_size("fsdp")
    return lax.ppermute(array, "fsdp", [(index, index ^ 1) for index in range(count)])


def pair(array):
    count = lax.axis_size("shard")
    return lax.ppermute(array, "shard", [(index, index ^ 1) for index in range(count)])


def far(array):
    count = lax.axis_size("shard")
    return lax.ppermute(array, "shard", [(index, index ^ 2) for index in range(count)])


def by_bit(bit, mine, other, axis):
    return jnp.where(
        bit == 0,
        jnp.concatenate([mine, other], axis=axis),
        jnp.concatenate([other, mine], axis=axis),
    )


def to_rows(piece, bit):
    mine = lax.dynamic_index_in_dim(piece, bit, axis=1, keepdims=False)
    other = core(lax.dynamic_index_in_dim(piece, 1 - bit, axis=1, keepdims=False))
    return by_bit(bit, mine, other, 0)


def from_rows(rows, bit):
    split = rows.reshape(2, rows.shape[0] // 2, rows.shape[1])
    mine = lax.dynamic_index_in_dim(split, bit, axis=0, keepdims=False)
    other = core(lax.dynamic_index_in_dim(split, 1 - bit, axis=0, keepdims=False))
    return by_bit(bit, mine[:, None], other[:, None], 1)


def plane_count():
    return lax.axis_size("fsdp") // 2


def plane_index():
    return lax.axis_index("fsdp") // 2


def plane(array, distance):
    count = lax.axis_size("fsdp")
    return lax.ppermute(
        array, "fsdp", [(index, index ^ (2 * distance)) for index in range(count)]
    )


def ring(array, distance):
    count = lax.axis_size("shard")
    return lax.ppermute(array, "shard", [(index, index ^ distance) for index in range(count)])


def gather_ring(array):
    others = {k: ring(array, k) for k in (3, 2, 1)}
    return [array] + [others[k] for k in range(1, BLOCKS)]


def return_ring(own, *sent):
    others = {k: ring(sent[k - 1], k) for k in (3, 2, 1)}
    return [own] + [others[k] for k in range(1, BLOCKS)]


def plane_groups():
    return [[2 * step + bit for step in range(plane_count())] for bit in range(2)]


def reorder(array):
    if plane_count() != PLANE:
        return array
    size = array.shape[-1] // PLANE
    index = plane_index()
    for step in (1, 2):
        blocks = [array[..., j * size : (j + 1) * size] for j in range(PLANE)]
        swapped = jnp.concatenate([blocks[j ^ step] for j in range(PLANE)], axis=-1)
        array = jnp.where((index & step) != 0, swapped, array)
    return array


def gather_pieces(rows):
    if plane_count() == PLANE:
        return [rows] + [plane(rows, k) for k in range(1, PLANE)]
    whole = lax.all_gather(rows, "fsdp", axis=0, axis_index_groups=plane_groups(), tiled=True)
    size = whole.shape[0] // PLANE
    return [whole[k * size : (k + 1) * size] for k in range(PLANE)]


def reduce_pieces(pieces):
    if plane_count() == PLANE:
        total = pieces[0].astype(F32)
        for k in range(1, PLANE):
            total = total + plane(pieces[k], k).astype(F32)
        return total
    return scatter_plane(jnp.concatenate(pieces, axis=0)).astype(F32)


def scatter_plane(whole):
    return lax.psum_scatter(
        whole, "fsdp", scatter_dimension=0, axis_index_groups=plane_groups(), tiled=True
    )


def hold(*values):
    return lax.optimization_barrier(values)


def gather_blocks(array):
    across = pair(array)
    return [array, core(array), across, core(across)]


def return_blocks(own, kept, sent):
    received = core(sent)
    count = own.shape[0]
    across = (kept + received[count:].astype(F32)).astype(BF16)
    return own, received, pair(across)


def pack_rows(*refs):
    out, rows = refs[-2:]
    rows[...] = jnp.zeros(rows.shape, rows.dtype)
    for row, ref in enumerate(refs[:-2]):
        rows[row : row + 1, : ref.shape[1]] = ref[...].astype(F32)
    out[...] = jnp.broadcast_to(rows[...].astype(out.dtype)[None], out.shape)


def run(kernel, outs, *operands, scratch=(), flops=0):
    spec = pl.BlockSpec(memory_space=pltpu.VMEM)
    moved = sum(o.size * o.dtype.itemsize for o in operands)
    moved += sum(functools.reduce(lambda a, b: a * b, shape) * 4 for shape, _ in outs)
    body = kernel.func if isinstance(kernel, functools.partial) else kernel
    return pl.pallas_call(
        kernel,
        out_shape=[jax.ShapeDtypeStruct(shape, kind) for shape, kind in outs],
        in_specs=[pl.BlockSpec(memory_space=pltpu.SMEM)] + [spec] * (len(operands) - 1),
        out_specs=[spec] * len(outs),
        scratch_shapes=list(scratch),
        cost_estimate=pl.CostEstimate(flops=flops, bytes_accessed=moved, transcendentals=0),
        name=body.__name__,
    )(*operands)


AT_PLANE, AT_SHARD, AT_FSDP, AT_COUNT = 0, 1, 2, 3


def mm(left, right, left_dim=1, right_dim=0):
    return lax.dot_general(
        left, right, (((left_dim,), (right_dim,)), ((), ())), preferred_element_type=F32
    )


def ordered(place, vec, row, swap):
    size = vec.shape[1] // PLANE
    blocks = []
    for j in range(PLANE):
        block = (place[AT_PLANE] ^ j) if swap else j
        blocks.append(vec[row : row + 1, pl.ds(pl.multiple_of(block * size, size), size)])
    return jnp.concatenate(blocks, axis=1)


def quarter_at(place, size, far_side):
    shard = place[AT_SHARD] ^ (2 if far_side else 0)
    return pl.multiple_of((shard * 2 + (place[AT_FSDP] & 1)) * size, size)


def unit_rows(values):
    center = values - jnp.mean(values, axis=-1, keepdims=True)
    scale = lax.rsqrt(jnp.mean(center * center, axis=-1, keepdims=True) + NORM_EPS)
    return center * scale, scale


def unit_back(unit, scale, grad_unit):
    mean_grad = jnp.mean(grad_unit, axis=-1, keepdims=True)
    mean_dot = jnp.mean(grad_unit * unit, axis=-1, keepdims=True)
    return scale * (grad_unit - mean_grad - unit * mean_dot)


def attn_forward(swap, place, vec, every, t0, t1, t2, t3, n0, n1, n2, n3, f0, f1, f2, f3,
                 act, qkv, probs, mixed, own, kept, sent):
    count = t0.shape[0]
    half = n0.shape[1] // 4
    width = vec.shape[1]
    size = width // PLANE
    gain, shift = ordered(place, vec, 0, swap), ordered(place, vec, 1, swap)
    for b, ref in enumerate((t0, t1, t2, t3)):
        unit, _ = unit_rows(ref[...].astype(F32))
        act[b * count : (b + 1) * count] = (unit * gain + shift).astype(BF16)
    for side, pieces in enumerate(((n0, n1, n2, n3), (f0, f1, f2, f3))):
        total = mm(act[:, :size], pieces[0][:, : 3 * half])
        for k in range(1, PLANE):
            total = total + mm(act[:, k * size : (k + 1) * size], pieces[k][:, : 3 * half])
        at = quarter_at(place, half, side == 1)
        bias = [vec[6:7, pl.ds(at, half)], jnp.zeros((1, half), F32), vec[7:8, pl.ds(at, half)]]
        total = total + jnp.concatenate(bias, axis=1)
        qkv[:, side * 3 * half : (side + 1) * 3 * half] = total.astype(BF16)
    keys = lax.broadcasted_iota(jnp.int32, (count, count), 0)
    queries = lax.broadcasted_iota(jnp.int32, (count, count), 1)

    def block(b, carry):
        rows = pl.ds(pl.multiple_of(b * count, count), count)
        device = (place[AT_FSDP] ^ (b & 1)) * place[AT_COUNT] + (place[AT_SHARD] ^ (b >> 1))
        starts = every[device].astype(F32)[9:10, :count].astype(jnp.int32)
        seen = (keys >= starts) & (keys <= queries)
        outs = []
        for h in range(BLOCKS):
            base = (h // 2) * 3 * half + (h % 2) * HEAD_DIM
            query = qkv[rows, base : base + HEAD_DIM]
            key = qkv[rows, base + half : base + half + HEAD_DIM]
            value = qkv[rows, base + 2 * half : base + 2 * half + HEAD_DIM]
            scores = jnp.where(seen, mm(key, query, 1, 1) * HEAD_DIM**-0.5, NEG_FILL)
            grown = jnp.exp(scores - jnp.max(scores, axis=0, keepdims=True))
            prob = grown / jnp.sum(grown, axis=0, keepdims=True)
            probs[b, h] = prob
            outs.append(mm(prob.astype(BF16), value, 0, 0))
        mixed[rows, :] = jnp.concatenate(outs, axis=1).astype(BF16)
        return carry

    lax.fori_loop(0, BLOCKS, block, 0, unroll=True)
    for k, (near, far_) in enumerate(zip((n0, n1, n2, n3), (f0, f1, f2, f3))):
        cols = slice(k * size, (k + 1) * size)
        part = mm(mixed[:, :half], near[:, 3 * half :], 1, 1)
        part = part + mm(mixed[:, half:], far_[:, 3 * half :], 1, 1)
        split_blocks(part, cols, count, own, kept, sent)


def split_blocks(part, cols, count, own, kept, sent):
    own[:, cols] = part[:count]
    kept[:, cols] = part[2 * count : 3 * count]
    sent[:count, cols] = part[count : 2 * count].astype(BF16)
    sent[count:, cols] = part[3 * count :].astype(BF16)


def natural(place, j, size, swap):
    return pl.ds(pl.multiple_of(((place[AT_PLANE] ^ j) if swap else j) * size, size), size)


def mlp_norm(swap, place, vec, tokens, own, received, across, hidden, hidden_natural, act):
    count, width = tokens.shape
    size = width // PLANE
    total = tokens[...].astype(F32) + ordered(place, vec, 2, swap)
    total = total + (own[...] + received[:count].astype(F32) + across[...].astype(F32))
    hidden[...] = total
    unit, _ = unit_rows(total)
    low = (unit * ordered(place, vec, 3, swap) + ordered(place, vec, 4, swap)).astype(BF16)
    for j in range(PLANE):
        there = natural(place, j, size, swap)
        act[:, there] = low[:, j * size : (j + 1) * size]
        hidden_natural[:, there] = total[:, j * size : (j + 1) * size]


def split_ring(part, cols, count, own, s1, s2, s3):
    own[:, cols] = part[:count]
    for k, ref in enumerate((s1, s2, s3)):
        ref[:, cols] = part[(k + 1) * count : (k + 2) * count].astype(BF16)


def shard_block(place, ref, distance, count):
    return ref[pl.ds(pl.multiple_of((place[AT_SHARD] ^ distance) * count, count), count)]


def mlp_forward(place, up_bias, both, a0, a1, a2, a3, grads, act_up, grad_pre,
                bias_sum, own, s1, s2, s3, act, grad):
    count, width = a0.shape
    units = both.shape[1] // 2
    tile = min(256, units)
    for b, act_ref in enumerate((a0, a1, a2, a3)):
        act[b * count : (b + 1) * count] = act_ref[...]
        grad[b * count : (b + 1) * count] = shard_block(place, grads, b, count)
    bias_sum[...] = jnp.zeros(bias_sum.shape, F32)
    start = place[AT_SHARD] * units

    def step(j, carry):
        inner = pl.ds(pl.multiple_of(j * tile, tile), tile)
        whole = pl.ds(pl.multiple_of(start + j * tile, tile), tile)
        second = pl.ds(pl.multiple_of(units + j * tile, tile), tile)
        pre = mm(act[...], both[:, inner]) + up_bias[:, whole]
        square = pre * pre
        bend = jnp.tanh(GELU_ROOT * (pre + GELU_CUBE * square * pre))
        half_in = 0.5 * (1.0 + bend)
        act_up[:, inner] = (pre * half_in).astype(BF16)
        slope = half_in + 0.5 * pre * (1.0 - bend * bend) * (
            GELU_ROOT * (1.0 + 3.0 * GELU_CUBE * square)
        )
        back = mm(grad[...], both[:, second]) * slope
        grad_pre[:, inner] = back.astype(BF16)
        bias_sum[:, whole] = jnp.sum(back, axis=0, keepdims=True)
        return carry

    lax.fori_loop(0, units // tile, step, 0)
    size = width // PLANE
    for k in range(PLANE):
        cols = slice(k * size, (k + 1) * size)
        split_ring(mm(grad_pre[...], both[cols, :units], 1, 1), cols, count, own, s1, s2, s3)


def unit_grads(swap, place, act_up, grad_pre, both, a0, a1, a2, a3, grads,
               g_down, g_up, g_up_sent, own, s1, s2, s3, rows):
    count, width = a0.shape
    half_units = g_up.shape[1] // 2
    size = width // PLANE
    for b in range(BLOCKS):
        rows[b * count : (b + 1) * count] = shard_block(place, grads, b, count)
    for side in range(2):
        cols = slice(side * half_units, (side + 1) * half_units)
        g_down[:, cols] = mm(rows[...], act_up[:, cols], 0, 0).astype(BF16)
    for b, ref in enumerate((a0, a1, a2, a3)):
        rows[b * count : (b + 1) * count] = ref[...]
    if swap:
        size = width // (2 * PLANE)
        for far_core in range(2):
            for k in range(PLANE):
                block = (place[AT_FSDP] ^ (2 * k)) ^ far_core
                there = pl.ds(pl.multiple_of(block * size, size), size)
                part = mm(rows[:, there], grad_pre[...], 0, 0).astype(BF16)
                (g_up_sent if far_core else g_up)[k * size : (k + 1) * size] = part
    else:
        for side, out in enumerate((g_up, g_up_sent)):
            cols = slice(side * width // 2, (side + 1) * width // 2)
            out[...] = mm(rows[:, cols], grad_pre[...], 0, 0).astype(BF16)
    size = width // PLANE
    for k in range(PLANE):
        cols = slice(k * size, (k + 1) * size)
        split_ring(mm(act_up[...], both[cols, act_up.shape[1] :], 1, 1), cols, count, own, s1, s2, s3)


def norm_back(swap, place, vec, hidden, grad_out, own, r1, r2, r3, grad_hidden, low, sums):
    width = hidden.shape[1]
    size = width // PLANE
    unit, scale = unit_rows(hidden[...])
    blocks = []
    for j in range(PLANE):
        there = natural(place, j, size, swap)
        block = own[:, there]
        for ref in (r1, r2, r3):
            block = block + ref[:, there].astype(F32)
        blocks.append(block)
    grad = jnp.concatenate(blocks, axis=1)
    total = grad_out[...] + unit_back(unit, scale, grad * ordered(place, vec, 3, swap))
    grad_hidden[...] = total
    low[...] = total.astype(BF16)
    sums[0:1] = jnp.sum(grad * unit, axis=0, keepdims=True)
    sums[1:2] = jnp.sum(grad, axis=0, keepdims=True)
    sums[2:3] = jnp.sum(total, axis=0, keepdims=True)
    sums[3:4] = jnp.sum(grad_out[...], axis=0, keepdims=True)


def attn_backward(place, qkv, probs, mixed, act, h0, h1, h2, h3, n0, n1, n2, n3, f0, f1, f2, f3,
                  far0, far1, far2, far3, near0, near1, near2, near3, low, bias_sum, grad,
                  grad_mixed):
    count, width = h0.shape
    size = width // PLANE
    half = n0.shape[1] // 4
    for b, ref in enumerate((h0, h1, h2, h3)):
        grad[b * count : (b + 1) * count] = ref[...]
    sides = ((n0, n1, n2, n3), (f0, f1, f2, f3))
    for side, pieces in enumerate(sides):
        total = mm(grad[:, :size], pieces[0][:, 3 * half :])
        for k in range(1, PLANE):
            total = total + mm(grad[:, k * size : (k + 1) * size], pieces[k][:, 3 * half :])
        grad_mixed[:, side * half : (side + 1) * half] = total.astype(BF16)
    bias_sum[...] = jnp.zeros(bias_sum.shape, F32)

    def block(b, sums):
        rows = pl.ds(pl.multiple_of(b * count, count), count)
        parts = [[], [], []]
        for h in range(BLOCKS):
            base = (h // 2) * 3 * half + (h % 2) * HEAD_DIM
            query = qkv[rows, base : base + HEAD_DIM]
            key = qkv[rows, base + half : base + half + HEAD_DIM]
            value = qkv[rows, base + 2 * half : base + 2 * half + HEAD_DIM]
            out = grad_mixed[rows, h * HEAD_DIM : (h + 1) * HEAD_DIM]
            prob = probs[b, h]
            back = mm(value, out, 1, 1)
            mean = jnp.sum(prob * back, axis=0, keepdims=True)
            scores = (prob * (back - mean) * HEAD_DIM**-0.5).astype(BF16)
            parts[0].append(mm(scores, key, 0, 0))
            parts[1].append(mm(scores, query, 1, 0))
            parts[2].append(mm(prob.astype(BF16), out, 1, 0))
        new = []
        for side in range(2):
            for which in range(3):
                joined = jnp.concatenate(parts[which][2 * side : 2 * side + 2], axis=1)
                base = (side * 3 + which) * half
                low[rows, base : base + half] = joined.astype(BF16)
                if which != 1:
                    new.append(jnp.sum(joined, axis=0, keepdims=True))
        return tuple(a + c for a, c in zip(sums, new))

    zero = jnp.zeros((1, half), F32)
    sums = lax.fori_loop(0, BLOCKS, block, (zero,) * 4, unroll=True)
    for side in range(2):
        at = quarter_at(place, half, side == 1)
        bias_sum[0:1, pl.ds(at, half)] = sums[2 * side]
        bias_sum[1:2, pl.ds(at, half)] = sums[2 * side + 1]
    for side, outs in ((1, (far0, far1, far2, far3)), (0, (near0, near1, near2, near3))):
        for k, out in enumerate(outs):
            cols = slice(k * size, (k + 1) * size)
            out[:, : 3 * half] = mm(
                act[:, cols], low[:, side * 3 * half : (side + 1) * 3 * half], 0, 0
            ).astype(BF16)
            out[:, 3 * half :] = mm(
                grad[:, cols], mixed[:, side * half : (side + 1) * half], 0, 0
            ).astype(BF16)


def attn_return(place, low, n0, n1, n2, n3, f0, f1, f2, f3, own, kept, sent):
    count = own.shape[0]
    half = n0.shape[1] // 4
    size = own.shape[1] // PLANE
    for k, (near, far_) in enumerate(zip((n0, n1, n2, n3), (f0, f1, f2, f3))):
        part = mm(low[:, : 3 * half], near[:, : 3 * half], 1, 1)
        part = part + mm(low[:, 3 * half :], far_[:, : 3 * half], 1, 1)
        split_blocks(part, slice(k * size, (k + 1) * size), count, own, kept, sent)


def input_back(swap, place, vec, tokens, grad_hidden, own, received, across, grad_in, sums):
    count = tokens.shape[0]
    unit, scale = unit_rows(tokens[...].astype(F32))
    grad = own[...] + received[:count].astype(F32) + across[...].astype(F32)
    gain = ordered(place, vec, 0, swap)
    grad_in[...] = grad_hidden[...] + unit_back(unit, scale, grad * gain)
    sums[0:1] = jnp.sum(grad * unit, axis=0, keepdims=True)
    sums[1:2] = jnp.sum(grad, axis=0, keepdims=True)


def on_device(
    tokens,
    cotangent,
    starts,
    counts,
    attn_gain,
    attn_shift,
    w_qkv,
    query_bias,
    value_bias,
    w_proj,
    proj_bias,
    mlp_gain,
    mlp_shift,
    w_up,
    up_bias,
    w_down,
    down_bias,
):
    slot_count, width = tokens.shape
    shard, fsdp = lax.axis_index("shard"), lax.axis_index("fsdp")
    shard_count, fsdp_count = lax.axis_size("shard"), lax.axis_size("fsdp")
    devices = shard_count * fsdp_count
    bit = fsdp % 2
    swap = plane_count() == PLANE
    place = jnp.stack([plane_index(), shard, fsdp, jnp.int32(shard_count)]).astype(jnp.int32)
    rows = w_qkv.shape[0]
    quarter = w_qkv.shape[2]
    half = quarter // 2
    units = w_up.shape[1]
    row_count = BLOCKS * slot_count

    with jax.named_scope("attn_weights"):
        attn_piece = jnp.concatenate(
            [
                jnp.transpose(w_qkv.reshape(rows, 3, 2, half), (0, 2, 1, 3)).reshape(
                    rows, 2, 3 * half
                ),
                w_proj.T.reshape(rows, 2, half),
            ],
            axis=2,
        )
        attn_near = to_rows(attn_piece, bit)
    with jax.named_scope("token_rows"):
        first, attn_near = hold(tokens, attn_near)
        token_low = reorder(first)
        token_across = pair(token_low)
    with jax.named_scope("attn_weights"):
        attn_far = far(attn_near)
        near = gather_pieces(attn_near)
    with jax.named_scope("vectors"):
        pieces = [
            v.reshape(1, -1)
            for v in (
                attn_gain,
                attn_shift,
                proj_bias,
                mlp_gain,
                mlp_shift,
                down_bias,
                query_bias,
                value_bias,
                up_bias,
                starts,
            )
        ]
        lanes = max(piece.shape[1] for piece in pieces)
        packed = pl.pallas_call(
            pack_rows,
            out_shape=jax.ShapeDtypeStruct((devices, 16, lanes), BF16),
            scratch_shapes=[pltpu.VMEM((16, lanes), F32)],
            name="pack_rows",
        )(*pieces)
    live = (jnp.arange(slot_count, dtype=jnp.int32) < counts[0]).astype(F32)[:, None]
    grad_natural = cotangent.astype(F32) * live
    grad_low = grad_natural.astype(BF16)
    grad_out = reorder(cotangent).astype(F32) * live
    mlp_piece = jnp.concatenate([w_up, w_down.T], axis=1)
    grad_low, attn_far, token_low, token_across, packed, place, mlp_piece, *near = hold(
        grad_low, attn_far, token_low, token_across, packed, place, mlp_piece, *near
    )
    with jax.named_scope("grad_rows"):
        grad_rows = lax.all_gather(grad_low, "shard", axis=0, tiled=True)
    with jax.named_scope("attn_weights"):
        away = gather_pieces(attn_far)
    with jax.named_scope("token_rows"):
        token_rows = [token_low, core(token_low), token_across, core(token_across)]
    with jax.named_scope("vectors"):
        every = lax.all_to_all(packed, ("fsdp", "shard"), 0, 0, tiled=True)
        grid = every.reshape(fsdp_count, shard_count, 16, lanes)
        size = attn_gain.shape[1]
        vec = jnp.transpose(grid[:, :, :8, :size], (2, 1, 0, 3)).reshape(8, -1).astype(F32)
        size = up_bias.shape[1]
        up_vec = jnp.transpose(grid[:, :, 8, :size], (1, 0, 2)).reshape(1, -1).astype(F32)
    every, vec, up_vec, mlp_piece, *held = hold(
        every, vec, up_vec, mlp_piece, *token_rows, *away
    )
    token_rows, away = held[:BLOCKS], held[BLOCKS:]
    with jax.named_scope("mlp_weights"):
        both = lax.all_gather(mlp_piece, "fsdp", axis=0, tiled=True)
    block = (slot_count, width)
    parts = [(block, F32), (block, F32), ((2 * slot_count, width), BF16)]
    act, qkv, probs, mixed, *attn_parts = run(
        functools.partial(attn_forward, swap),
        [
            ((row_count, width), BF16),
            ((row_count, 3 * quarter), BF16),
            ((BLOCKS, BLOCKS, slot_count, slot_count), F32),
            ((row_count, quarter), BF16),
            *parts,
        ],
        place,
        vec,
        every,
        *token_rows,
        *near,
        *away,
    )
    with jax.named_scope("attn_return"):
        attn_term = return_blocks(*attn_parts)
    hidden, hidden_natural, mlp_act = run(
        functools.partial(mlp_norm, swap),
        [(block, F32), (block, F32), (block, BF16)],
        place,
        vec,
        token_low,
        *attn_term,
    )
    with jax.named_scope("mlp_inputs"):
        mlp_rows = gather_ring(mlp_act)
    whole = pltpu.VMEM((row_count, width), BF16)
    ring_parts = [(block, F32)] + [(block, BF16)] * (BLOCKS - 1)
    act_up, grad_pre, up_bias_sum, *normed_parts = run(
        mlp_forward,
        [((row_count, units), BF16), ((row_count, units), BF16), (up_vec.shape, F32), *ring_parts],
        place,
        up_vec,
        both,
        *mlp_rows,
        grad_rows,
        scratch=[whole, whole],
    )
    with jax.named_scope("normed_return"):
        grad_normed = return_ring(*normed_parts)
    half_rows = ((width // 2, units), BF16)
    g_down, g_up, g_up_sent, *mlp_parts = run(
        functools.partial(unit_grads, swap),
        [((width, units), BF16), half_rows, half_rows, *ring_parts],
        place,
        act_up,
        grad_pre,
        both,
        *mlp_rows,
        grad_rows,
        scratch=[whole],
    )
    with jax.named_scope("down_grads"):
        g_down_own = lax.psum_scatter(g_down, "fsdp", scatter_dimension=0, tiled=True)
    g_down, g_up, g_up_sent, *held = hold(g_down, g_up, g_up_sent, *mlp_parts, *grad_normed)
    mlp_parts, grad_normed = held[:BLOCKS], held[BLOCKS:]
    grad_hidden, hidden_low, sums = run(
        functools.partial(norm_back, swap),
        [(block, F32), (block, BF16), ((4, width), F32)],
        place,
        vec,
        hidden,
        grad_out,
        *grad_normed,
    )
    with jax.named_scope("up_grads"):
        if swap:
            others = core(g_up_sent)
            g_up_half = []
            for k in range(PLANE):
                piece = slice(k * rows, (k + 1) * rows)
                g_up_half.append((g_up[piece].astype(F32) + others[piece].astype(F32)).astype(BF16))
        else:
            g_up_half = [jnp.concatenate([g_up, g_up_sent], axis=0)]
    with jax.named_scope("hidden_rows"):
        across, *g_up_half = hold(pair(hidden_low), *g_up_half)
        hidden_rows = [hidden_low, core(hidden_low), across, core(across)]
    with jax.named_scope("up_grads"):
        if swap:
            g_up_parts = g_up_half[:1] + [plane(g_up_half[k], k) for k in range(1, PLANE)]
        else:
            g_up_parts = [lax.psum_scatter(g_up_half[0], "fsdp", scatter_dimension=0, tiled=True)]
    with jax.named_scope("mlp_return"):
        mlp_own, *mlp_others = return_ring(*mlp_parts)
    side = ((width // PLANE, 4 * half), BF16)
    *held, low, bias_sum = run(
        attn_backward,
        [side] * (2 * PLANE) + [((row_count, 3 * quarter), BF16), ((2, width), F32)],
        place,
        qkv,
        probs,
        mixed,
        act,
        *hidden_rows,
        *near,
        *away,
        scratch=[whole, pltpu.VMEM((row_count, quarter), BF16)],
    )
    g_attn_far, g_attn_near = held[:PLANE], held[PLANE:]
    back_parts = run(attn_return, parts, place, low, *near, *away)
    m1, m2, *held = hold(
        *mlp_others[:2], *back_parts, *g_up_parts, *g_attn_far, *g_attn_near
    )
    mlp_others = [m1, m2, *mlp_others[2:]]
    back_parts, g_up_parts, held = held[:3], held[3 : -2 * PLANE], held[-2 * PLANE :]
    g_attn_far, g_attn_near = held[:PLANE], held[PLANE:]
    with jax.named_scope("attn_grads"):
        g_attn_far = reduce_pieces(g_attn_far).astype(BF16)
    with jax.named_scope("attn_back"):
        grad_attn = return_blocks(*back_parts)
    g_attn_far, g_down_own, *held = hold(
        g_attn_far, g_down_own, *g_attn_near, *grad_attn, *mlp_others[:2]
    )
    g_attn_near, held = held[:PLANE], held[PLANE:]
    grad_attn, mlp_others = held[:3], [*held[3:], mlp_others[2]]
    with jax.named_scope("up_grads"):
        g_up = sum(part.astype(F32) for part in g_up_parts)
    with jax.named_scope("attn_grads"):
        if swap:
            near_parts = g_attn_near[:1] + [plane(g_attn_near[k], k) for k in range(1, PLANE)]
        else:
            near_parts = [scatter_plane(jnp.concatenate(g_attn_near, axis=0))]
        g_attn_far = far(g_attn_far)
    with jax.named_scope("mlp_return"):
        mlp_term = mlp_own + sum(part.astype(F32) for part in mlp_others)
    block_out = ((hidden_natural + mlp_term + vec[5:6]) * live).astype(BF16)
    grad_in, in_sums = run(
        functools.partial(input_back, swap),
        [(block, F32), ((2, width), F32)],
        place,
        vec,
        token_low,
        grad_hidden,
        *grad_attn,
    )
    with jax.named_scope("small_grads"):
        flat = jnp.concatenate([reorder(jnp.concatenate([in_sums, sums], axis=0)), bias_sum])
        flat = flat.reshape(8, shard_count, fsdp_count, -1)
        flat = jnp.transpose(flat, (2, 1, 0, 3)).reshape(devices, -1)
        size = up_bias.shape[1]
        upper = jnp.transpose(up_bias_sum.reshape(shard_count, fsdp_count, size), (1, 0, 2))
        small = jnp.concatenate([flat, upper.reshape(devices, size)], axis=1)
        small, near_parts[-1] = hold(small, near_parts[-1])
        small = jnp.sum(lax.all_to_all(small, ("fsdp", "shard"), 0, 0, tiled=True), axis=0)
        size = attn_gain.shape[1]
        g_vec = small[: 8 * size].reshape(8, 1, size)
        g_up_bias = small[8 * size :].reshape(1, -1)
    with jax.named_scope("attn_grads"):
        g_attn_near = sum(part.astype(F32) for part in near_parts)
        g_attn = from_rows((g_attn_near + g_attn_far.astype(F32)).astype(BF16), bit).astype(F32)
    g_qkv = jnp.transpose(g_attn[:, :, : 3 * half].reshape(rows, 2, 3, half), (0, 2, 1, 3))
    return (
        block_out,
        reorder(grad_in),
        g_vec[0],
        g_vec[1],
        g_qkv.reshape(w_qkv.shape),
        g_vec[6],
        g_vec[7],
        g_attn[:, :, 3 * half :].reshape(rows, quarter).T,
        g_vec[4],
        g_vec[2],
        g_vec[3],
        g_up,
        g_up_bias,
        g_down_own.astype(F32).T,
        g_vec[5],
    )


def solution(mesh):
    in_specs = (
        P(("fsdp", "shard"), None),
        P(("fsdp", "shard"), None),
        P(("fsdp", "shard")),
        P(("fsdp", "shard")),
        P("shard", "fsdp"),
        P("shard", "fsdp"),
        P("fsdp", None, "shard"),
        P("shard", "fsdp"),
        P("shard", "fsdp"),
        P("shard", "fsdp"),
        P("shard", "fsdp"),
        P("shard", "fsdp"),
        P("shard", "fsdp"),
        P("fsdp", "shard"),
        P("shard", "fsdp"),
        P("shard", "fsdp"),
        P("shard", "fsdp"),
    )
    out_specs = (
        P(("fsdp", "shard"), None),
        P(("fsdp", "shard"), None),
        P("shard", "fsdp"),
        P("shard", "fsdp"),
        P("fsdp", None, "shard"),
        P("shard", "fsdp"),
        P("shard", "fsdp"),
        P("shard", "fsdp"),
        P("shard", "fsdp"),
        P("shard", "fsdp"),
        P("shard", "fsdp"),
        P("fsdp", "shard"),
        P("shard", "fsdp"),
        P("shard", "fsdp"),
        P("shard", "fsdp"),
    )
    return jax.shard_map(
        on_device, mesh=mesh, in_specs=in_specs, out_specs=out_specs, check_vma=False
    )
```
